512 devices in a mesh: seq: 32 (over z, x), rep: 16 (over y, core).
Axes of the slice: x: 4, y: 8, z: 8, core: 2. Of those that a mesh axis runs over, the one named last changes fastest.
Arguments:
- states: bfloat16 [98304, 512], P(('rep', 'seq')), parts along dimension 0, may hold values from -6 to 6
- starts: int32 [16384], P(('rep', 'seq')), parts along dimension 0, may hold values from 0 to 6143, as said below
- straddle: int32 [512], P(('rep', 'seq')), parts along dimension 0, may hold values from 0 to 63, as said below
- key_weight: bfloat16 [512, 512], replicated
- out_weight: bfloat16 [512, 4096], P(None, 'seq'), may hold values from -0.25 to 0.25
- norm_gain: bfloat16 [4096], P('seq'), may hold values from 0.25 to 1.75
- attn_weight: bfloat16 [4096, 3, 4096], P(None, None, 'seq')
Outputs:
- attended: bfloat16 [16384, 4096], P(('rep', 'seq')), parts along dimension 0
The draws below stay inside these ranges and needn't reach their ends.
There are 16 independent parts, one for each index of `rep`. The reference program is written for one: setup_inputs(seed, part) draws one part's arguments, and reference() takes and returns one part's arrays. A program takes and returns all parts, laid end to end along the dimension named above; an argument that names none is the same for every part. Nothing has to cross between parts.
Inputs may be any that keep to these rules, and one draw needn't show every extreme that they name: Rising; shard s of 192 bytes holds the starts of exactly 32 patches, numbers s * 32 to (s+1) * 32 - 1; the first of them lies at most 63 bytes into the shard, and at byte 0 for shard 0. `straddle`: entry s equals the first start of shard s+1 minus (s+1) * 192; the last entry is 0.
All inputs are finite; a program needn't handle non-finite values.
Results may differ from the reference program's by a relative error of at most 0.0096.
Values may be sent and summed in bfloat16 or wider, within the bound.
No kernel may reach another device: no remote copies, remote signals or barrier semaphores. Data moves between devices by JAX's collectives and lax.ppermute only.
A program may use at most 64 MiB of HBM per device.

```python
import jax
import jax.numpy as jnp
from jax import lax

D = 4096
HD = 128
LD = 512
LHD = 128
B_DEV = 192
P_DEV = 32
HALO = 64
H = 32
LH = 4
SHARDS = 32
NB = 6144
NP = 1024


def patch_layout(key):
    shard_count = NP // P_DEV
    first_key, pick_key, other_key = jax.random.split(jax.random.fold_in(key, 7), 3)
    offsets = jax.random.randint(first_key, (shard_count,), 0, HALO)
    chosen = jax.random.randint(pick_key, (), 1, shard_count)
    shard_ids = jnp.arange(shard_count)
    offsets = jnp.where(shard_ids == chosen, HALO - 1, offsets)
    offsets = jnp.where(shard_ids == 0, 0, offsets)

    def others(sub_key):
        picked = jax.random.permutation(sub_key, B_DEV - HALO)[:P_DEV - 1]
        return jnp.sort(picked) + HALO
    extra = jax.vmap(others)(jax.random.split(other_key, shard_count))
    extra = extra.at[shard_count - 1, P_DEV - 2].set(B_DEV - 1)
    local = jnp.concatenate([offsets[:, None], extra], axis=1)
    starts = (local + shard_ids[:, None] * B_DEV).reshape(NP).astype(jnp.int32)
    straddle = jnp.concatenate([offsets[1:], jnp.zeros((1,), offsets.dtype)]).astype(jnp.int32)
    return (starts, straddle)


def draw_starts(key, part):
    return patch_layout(key)[0]


def draw_straddle(key, part):
    return patch_layout(key)[1]


def draw_key_weight(key, part):
    first_key = jax.random.fold_in(jax.random.fold_in(key, 11), 0)
    noise = jax.random.normal(first_key, (LD, LD), jnp.float32) * LD ** (-0.5)
    result = noise
    return result.astype(jnp.bfloat16)


def draw_attn_weight(key, part):
    first_key, second_key, third_key = jax.random.split(jax.random.fold_in(key, 13), 3)
    spread = D ** (-0.5)
    query_part = jax.random.normal(first_key, (D, D), jnp.float32) * spread
    value_part = jax.random.normal(third_key, (D, D), jnp.float32) * spread
    key_part = jax.random.normal(second_key, (D, D), jnp.float32) * spread
    return jnp.stack([query_part, key_part, value_part], axis=1).astype(jnp.bfloat16)


def steps_of(own_key, shape, cuts, least, largest):
    level, own = 1.0, jax.random.fold_in(own_key, 6)
    for dim, shards_of in cuts:
        heights = jnp.exp(jax.random.uniform(jax.random.fold_in(own, dim), (shards_of,), jnp.float32, least / len(cuts), largest / len(cuts)))
        level = level * jnp.repeat(heights, shape[dim] // shards_of).reshape([-1 if axis == dim else 1 for axis in range(len(shape))])
    return level


def scatter_about(rng, extent, scale, most, cuts=(), kind=jnp.bfloat16):
    entries = jax.random.normal(rng, extent, jnp.float32) * scale
    if len(cuts) > 0:
        entries = steps_of(rng, extent, cuts, -0.22, 0.18) * entries
    return jnp.clip(entries, min=-most, max=most).astype(kind)


def setup_inputs(seed: int = 0, part: int = 0) -> dict:
    arg_keys = jax.random.split(jax.random.key(seed), 8)
    part_splits = jax.random.split(jax.random.fold_in(arg_keys[7], part), 8)
    return {
        "states": scatter_about(part_splits[0], (NB, LD), 1.0, 6.0, ((0, 32),)),
        "starts": draw_starts(jax.random.fold_in(jax.random.fold_in(arg_keys[7], part), 71), part),
        "straddle": draw_straddle(jax.random.fold_in(jax.random.fold_in(arg_keys[7], part), 71), part),
        "key_weight": draw_key_weight(jax.random.fold_in(arg_keys[7], 71), part),
        "out_weight": scatter_about(arg_keys[4], (LD, D), LD ** -0.5, 0.25, ((1, 32),)),
        "norm_gain": jnp.clip(1.0 + 0.15 * jax.random.normal(arg_keys[5], (D,), jnp.float32), 0.25, 1.75).astype(jnp.bfloat16),
        "attn_weight": draw_attn_weight(jax.random.fold_in(arg_keys[7], 71), part),
    }


epsilon = 1e-05

def cross_pool(window, local_starts, halo_count, key_weight):
    window_rows = window.shape[0]
    position = jnp.arange(window_rows, dtype=jnp.int32)
    patch_ends = jnp.concatenate([local_starts[1:], (B_DEV + halo_count).reshape(1).astype(jnp.int32)])
    member = (position[None, :] >= local_starts[:, None]) & (position[None, :] < patch_ends[:, None])
    byte_count = lax.optimization_barrier(jnp.sum(member.astype(jnp.float32), axis=1))
    query = (jnp.dot(member.astype(jnp.bfloat16), window, preferred_element_type=jnp.float32) / byte_count[:, None]).astype(jnp.bfloat16)
    keys = jnp.dot(window, key_weight, preferred_element_type=jnp.float32).astype(jnp.bfloat16)
    query_heads = query.astype(jnp.float32).reshape(P_DEV, LH, LHD)
    key_heads = keys.astype(jnp.float32).reshape(window_rows, LH, LHD)
    scores = jnp.einsum('phd,jhd->hpj', query_heads, key_heads) / jnp.sqrt(jnp.float32(LHD))
    scores = jnp.where(member[None], scores, jnp.float32(-1e+30))
    row_peak = lax.optimization_barrier(jnp.max(scores, axis=-1, keepdims=True))
    expo = jnp.where(member[None], jnp.exp(scores - row_peak), jnp.float32(0.0))
    cross = (expo / lax.optimization_barrier(jnp.sum(expo, axis=-1, keepdims=True))).astype(jnp.bfloat16)
    value_heads = window.astype(jnp.float32).reshape(window_rows, LH, LHD)
    pooled = jnp.einsum('hpj,jhd->phd', cross.astype(jnp.float32), value_heads)
    return pooled.reshape(P_DEV, LD).astype(jnp.bfloat16)

def reference(states, starts, straddle, key_weight, out_weight, norm_gain, attn_weight):
    padded = jnp.concatenate([states, jnp.zeros((HALO, LD), states.dtype)], axis=0)
    start_table = starts.reshape(SHARDS, P_DEV)

    def one_shard(shard):
        window = lax.dynamic_slice_in_dim(padded, (shard * B_DEV).astype(jnp.int32), B_DEV + HALO, 0)
        local_starts = (start_table[shard] - shard * B_DEV).astype(jnp.int32)
        return cross_pool(window, local_starts, straddle[shard], key_weight)
    pooled = lax.map(one_shard, jnp.arange(SHARDS, dtype=jnp.int32)).reshape(NP, LD)
    embedding = jnp.dot(pooled, out_weight, preferred_element_type=jnp.float32)
    meansq = lax.optimization_barrier(jnp.mean(embedding * embedding, axis=1, keepdims=True))
    normed = (embedding * lax.rsqrt(meansq + epsilon) * norm_gain.astype(jnp.float32)[None, :]).astype(jnp.bfloat16)
    projected = jnp.dot(normed, attn_weight.reshape(D, 3 * D), preferred_element_type=jnp.float32).astype(jnp.bfloat16)
    head_view = projected.astype(jnp.float32).reshape(NP, 3, H, HD)
    scores = jnp.einsum('qhd,khd->hqk', head_view[:, 0], head_view[:, 1]) / jnp.sqrt(jnp.float32(HD))
    causal = jnp.arange(NP)[:, None] >= jnp.arange(NP)[None, :]
    scores = jnp.where(causal[None], scores, jnp.float32(-1e+30))
    row_peak = lax.optimization_barrier(jnp.max(scores, axis=-1, keepdims=True))
    expo = jnp.where(causal[None], jnp.exp(scores - row_peak), jnp.float32(0.0))
    probs = (expo / lax.optimization_barrier(jnp.sum(expo, axis=-1, keepdims=True))).astype(jnp.bfloat16)
    attended = jnp.einsum('hqk,khd->qhd', probs.astype(jnp.float32), head_view[:, 2])
    return attended.reshape(NP, D).astype(jnp.bfloat16)
```

```python
import jax
import jax.numpy as jnp
from jax import lax
from jax.sharding import PartitionSpec as P

HD = 128
LHD = 128
HALO = 64


epsilon = 1e-05


def shifted(shard, axis, by):
    size = lax.axis_size(axis)
    pairs = [(i, i + by) for i in range(size) if 0 <= i + by < size]
    return lax.ppermute(shard, axis, pairs)


def cross_pool(window, local_starts, halo_count, key_weight, patch_total, head_size):
    window_rows = window.shape[0]
    shard_bytes = window_rows - HALO
    width = window.shape[1]
    head_count = width // head_size
    position = jnp.arange(window_rows, dtype=jnp.int32)
    patch_ends = jnp.concatenate([local_starts[1:], (shard_bytes + halo_count).reshape(1)])
    member = (position[None, :] >= local_starts[:, None]) & (
        position[None, :] < patch_ends[:, None]
    )
    byte_count = jnp.sum(member.astype(jnp.float32), axis=1)
    query = (
        jnp.dot(member.astype(jnp.bfloat16), window, preferred_element_type=jnp.float32)
        / byte_count[:, None]
    ).astype(jnp.bfloat16)
    keys = jnp.dot(window, key_weight, preferred_element_type=jnp.float32).astype(jnp.bfloat16)
    query_heads = query.reshape(patch_total, head_count, head_size)
    key_heads = keys.reshape(window_rows, head_count, head_size)
    scores = jnp.einsum(
        "phd,jhd->hpj", query_heads, key_heads, preferred_element_type=jnp.float32
    ) / jnp.sqrt(jnp.float32(head_size))
    scores = jnp.where(member[None], scores, jnp.float32(-1e30))
    row_peak = jnp.max(scores, axis=-1, keepdims=True)
    expo = jnp.where(member[None], jnp.exp(scores - row_peak), jnp.float32(0.0))
    cross = (expo / jnp.sum(expo, axis=-1, keepdims=True)).astype(jnp.bfloat16)
    value_heads = window.reshape(window_rows, head_count, head_size)
    pooled = jnp.einsum("hpj,jhd->phd", cross, value_heads, preferred_element_type=jnp.float32)
    return pooled.reshape(patch_total, width).astype(jnp.bfloat16)


def global_attend(head_view):
    patch_count = head_view.shape[0]
    scores = jnp.einsum(
        "qhd,khd->hqk", head_view[:, 0], head_view[:, 1], preferred_element_type=jnp.float32
    ) / jnp.sqrt(jnp.float32(HD))
    causal = jnp.arange(patch_count)[:, None] >= jnp.arange(patch_count)[None, :]
    scores = jnp.where(causal[None], scores, jnp.float32(-1e30))
    row_peak = jnp.max(scores, axis=-1, keepdims=True)
    expo = jnp.where(causal[None], jnp.exp(scores - row_peak), jnp.float32(0.0))
    probs = (expo / jnp.sum(expo, axis=-1, keepdims=True)).astype(jnp.bfloat16)
    attended = jnp.einsum(
        "hqk,khd->qhd", probs, head_view[:, 2], preferred_element_type=jnp.float32
    )
    return attended.reshape(patch_count, head_view.shape[2] * HD).astype(jnp.bfloat16)


def spread(block, axis):
    copies = jnp.broadcast_to(block[None], (lax.axis_size(axis),) + block.shape)
    return lax.all_to_all(copies, axis, split_axis=0, concat_axis=0, tiled=True)


def shards(states, starts, straddle, key_weight, out_weight, norm_gain, attn_weight):
    shard_index = lax.axis_index("seq")
    byte_rows = states.shape[0]
    patch_local = starts.shape[0]
    local_width = attn_weight.shape[2]
    model_width = attn_weight.shape[0]
    pooled_width = out_weight.shape[0]

    piece = pooled_width // lax.axis_size("rep")
    rows = lax.dynamic_slice_in_dim(out_weight, lax.axis_index("rep") * piece, piece, 0)
    gain_block = jnp.broadcast_to(norm_gain[None], (8, norm_gain.shape[0]))
    weight_blocks = spread(jnp.concatenate([rows, gain_block], axis=0), "seq")
    row_block = weight_blocks[:, :piece].astype(jnp.float32)
    gain = weight_blocks[:, piece : piece + 1].astype(jnp.float32)
    scaled = jnp.swapaxes(row_block * gain, 0, 1).reshape(piece, model_width)
    scaled_high = scaled.astype(jnp.bfloat16)
    scaled_low = (scaled - scaled_high.astype(jnp.float32)).astype(jnp.bfloat16)
    proj_weight = attn_weight.reshape(model_width, 3 * local_width)
    merged = jnp.dot(
        jnp.concatenate([scaled_high, scaled_low], axis=0),
        proj_weight,
        preferred_element_type=jnp.float32,
    )
    merged = (merged[:piece] + merged[piece:]).astype(jnp.bfloat16)
    merged_all = spread(merged, "rep").reshape(pooled_width, 3 * local_width)

    halo_rows = shifted(states[:HALO], "seq", -1)
    window = jnp.concatenate([states, halo_rows], axis=0)
    local_starts = starts - shard_index * byte_rows
    pooled = cross_pool(window, local_starts, straddle[0], key_weight, patch_local, LHD)
    pooled_all = spread(pooled, "seq").reshape(-1, pooled_width)

    part = lax.dot_general(
        out_weight, pooled_all, (((0,), (1,)), ((), ())), preferred_element_type=jnp.float32
    )
    part_square = jnp.sum(part * part, axis=0).reshape(-1, 128)
    square = jnp.sum(spread(part_square, "seq"), axis=0).reshape(-1)
    inverse = lax.rsqrt(square / model_width + epsilon)
    projected = (
        jnp.dot(pooled_all, merged_all, preferred_element_type=jnp.float32) * inverse[:, None]
    ).astype(jnp.bfloat16)
    head_view = projected.reshape(projected.shape[0], 3, local_width // HD, HD)
    attended = global_attend(head_view)
    return lax.all_to_all(attended, "seq", split_axis=0, concat_axis=1, tiled=True)


def solution(mesh):
    placed = (
        P(("rep", "seq"), None),
        P(("rep", "seq")),
        P(("rep", "seq")),
        P(),
        P(None, "seq"),
        P("seq"),
        P(None, None, "seq"),
    )
    return jax.shard_map(
        shards, mesh=mesh, in_specs=placed, out_specs=P(("rep", "seq"), None), check_vma=False
    )
```

```python
import jax
import jax.numpy as jnp
from jax import lax
from jax.sharding import PartitionSpec as P


HD = 128
LHD = 128
HALO = 64


epsilon = 1e-05


def shifted(shard, axis, by):
    size = lax.axis_size(axis)
    pairs = [(i, i + by) for i in range(size) if 0 <= i + by < size]
    return lax.ppermute(shard, axis, pairs)


def cross_pool(window, local_starts, halo_count, key_weight, patch_total, head_size):
    window_rows = window.shape[0]
    shard_bytes = window_rows - HALO
    width = window.shape[1]
    head_count = width // head_size
    position = jnp.arange(window_rows, dtype=jnp.int32)
    patch_ends = jnp.concatenate([local_starts[1:], (shard_bytes + halo_count).reshape(1)])
    member = (position[None, :] >= local_starts[:, None]) & (
        position[None, :] < patch_ends[:, None]
    )
    byte_count = jnp.sum(member.astype(jnp.float32), axis=1)
    query = (
        jnp.dot(member.astype(jnp.bfloat16), window, preferred_element_type=jnp.float32)
        / byte_count[:, None]
    ).astype(jnp.bfloat16)
    keys = jnp.dot(window, key_weight, preferred_element_type=jnp.float32).astype(jnp.bfloat16)
    query_heads = query.reshape(patch_total, head_count, head_size)
    key_heads = keys.reshape(window_rows, head_count, head_size)
    scores = jnp.einsum(
        "phd,jhd->hpj", query_heads, key_heads, preferred_element_type=jnp.float32
    ) / jnp.sqrt(jnp.float32(head_size))
    scores = jnp.where(member[None], scores, jnp.float32(-1e30))
    row_peak = jnp.max(scores, axis=-1, keepdims=True)
    expo = jnp.where(member[None], jnp.exp(scores - row_peak), jnp.float32(0.0))
    cross = (expo / jnp.sum(expo, axis=-1, keepdims=True)).astype(jnp.bfloat16)
    value_heads = window.reshape(window_rows, head_count, head_size)
    pooled = jnp.einsum("hpj,jhd->phd", cross, value_heads, preferred_element_type=jnp.float32)
    return pooled.reshape(patch_total, width).astype(jnp.bfloat16)


def global_attend(head_view):
    patch_count = head_view.shape[0]
    scores = jnp.einsum(
        "qhd,khd->hqk", head_view[:, 0], head_view[:, 1], preferred_element_type=jnp.float32
    ) / jnp.sqrt(jnp.float32(HD))
    causal = jnp.arange(patch_count)[:, None] >= jnp.arange(patch_count)[None, :]
    scores = jnp.where(causal[None], scores, jnp.float32(-1e30))
    row_peak = jnp.max(scores, axis=-1, keepdims=True)
    expo = jnp.where(causal[None], jnp.exp(scores - row_peak), jnp.float32(0.0))
    probs = (expo / jnp.sum(expo, axis=-1, keepdims=True)).astype(jnp.bfloat16)
    attended = jnp.einsum(
        "hqk,khd->qhd", probs, head_view[:, 2], preferred_element_type=jnp.float32
    )
    return attended.reshape(patch_count, head_view.shape[2] * HD).astype(jnp.bfloat16)


def spread(block, axis):
    copies = jnp.broadcast_to(block[None], (lax.axis_size(axis),) + block.shape)
    return lax.all_to_all(copies, axis, split_axis=0, concat_axis=0, tiled=True)


def weight_rows(out_weight, norm_gain):
    piece = out_weight.shape[0] // lax.axis_size("rep")
    rows = lax.dynamic_slice_in_dim(out_weight, lax.axis_index("rep") * piece, piece, 0)
    gain_block = jnp.broadcast_to(norm_gain[None], (8, norm_gain.shape[0]))
    return jnp.concatenate([rows, gain_block], axis=0)


def merge_weights(weight_blocks, attn_weight):
    model_width = attn_weight.shape[0]
    piece = weight_blocks.shape[1] - 8
    row_block = weight_blocks[:, :piece].astype(jnp.float32)
    gain = weight_blocks[:, piece : piece + 1].astype(jnp.float32)
    scaled = jnp.swapaxes(row_block * gain, 0, 1).reshape(piece, model_width)
    high = scaled.astype(jnp.bfloat16)
    low = (scaled - high.astype(jnp.float32)).astype(jnp.bfloat16)
    both = jnp.concatenate([high, low], axis=0)
    merged = [
        jnp.dot(both, attn_weight[:, part], preferred_element_type=jnp.float32)
        for part in range(3)
    ]
    merged = jnp.concatenate([m[:piece] + m[piece:] for m in merged], axis=1)
    return merged.astype(jnp.bfloat16)


def layer(states, starts, straddle, key_weight, out_weight, norm_gain, attn_weight):
    shard_index = lax.axis_index("seq")
    byte_rows = states.shape[0]
    patch_local = starts.shape[0]
    model_width = attn_weight.shape[0]
    pooled_width = out_weight.shape[0]

    weight_blocks = spread(weight_rows(out_weight, norm_gain), "seq")
    halo_rows = shifted(states[:HALO], "seq", -1)
    window = jnp.concatenate([states, halo_rows], axis=0)
    local_starts = starts - shard_index * byte_rows
    pooled = cross_pool(window, local_starts, straddle[0], key_weight, patch_local, LHD)
    pooled_all = spread(pooled, "seq").reshape(-1, pooled_width)
    merged = merge_weights(weight_blocks, attn_weight)
    merged_all = lax.all_gather(merged, "rep", axis=0, tiled=True)
    part = lax.dot_general(
        out_weight, pooled_all, (((0,), (1,)), ((), ())), preferred_element_type=jnp.float32
    )
    part_square = jnp.sum(part * part, axis=0).reshape(-1, 128)
    square_all = spread(part_square, "seq")
    square = jnp.sum(square_all, axis=0).reshape(-1)
    inverse = lax.rsqrt(square / model_width + epsilon)
    projected = (
        jnp.dot(pooled_all, merged_all, preferred_element_type=jnp.float32) * inverse[:, None]
    ).astype(jnp.bfloat16)
    head_view = projected.reshape(projected.shape[0], 3, -1, HD)
    attended = global_attend(head_view)
    return lax.all_to_all(attended, "seq", split_axis=0, concat_axis=1, tiled=True)


def solution(mesh):
    placed = (
        P(("rep", "seq"), None),
        P(("rep", "seq")),
        P(("rep", "seq")),
        P(),
        P(None, "seq"),
        P("seq"),
        P(None, None, "seq"),
    )
    return jax.shard_map(
        layer, mesh=mesh, in_specs=placed, out_specs=P(("rep", "seq"), None), check_vma=False
    )
```

```python
import functools

import jax
import jax.numpy as jnp
from jax import lax
from jax.experimental import pallas as pl
from jax.experimental.pallas import tpu as pltpu
from jax.sharding import PartitionSpec as P


HD = 128
LHD = 128
HALO = 64
ROWS = 32
GAIN_ROWS = 8
TILE = 256


epsilon = 1e-05


def shifted(shard, axis, by):
    size = lax.axis_size(axis)
    pairs = [(i, i + by) for i in range(size) if 0 <= i + by < size]
    return lax.ppermute(shard, axis, pairs)


def whole(count):
    return [pl.BlockSpec(memory_space=pltpu.VMEM)] * count


def scalars(count):
    return [pl.BlockSpec(memory_space=pltpu.SMEM)] * count


def rows_kernel(index_ref, weight_ref, gain_ref, out_ref):
    start = pl.multiple_of(index_ref[0] * ROWS, ROWS)
    rows = weight_ref[pl.ds(start, ROWS), :]
    gain = jnp.broadcast_to(gain_ref[...], (GAIN_ROWS, gain_ref.shape[1]))
    block = jnp.concatenate([rows, gain], axis=0)
    for target in range(out_ref.shape[0]):
        out_ref[target] = block


def weight_rows(out_weight, norm_gain, index, copies):
    return pl.pallas_call(
        rows_kernel,
        out_shape=jax.ShapeDtypeStruct((copies, ROWS + GAIN_ROWS, out_weight.shape[1]), jnp.bfloat16),
        in_specs=scalars(1) + whole(2),
        out_specs=pl.BlockSpec(memory_space=pltpu.VMEM),
        name="rows",
    )(index.reshape(1), out_weight, norm_gain.reshape(1, -1))


def keys_kernel(base_ref, starts_ref, straddle_ref, states_ref, weight_ref, keys_ref, first_ref, end_ref, states_out, weight_out):
    patches = first_ref.shape[0]
    shard_bytes = states_ref.shape[0]
    keys_ref[...] = jnp.dot(
        states_ref[...], weight_ref[...], preferred_element_type=jnp.float32
    ).astype(jnp.bfloat16)
    states_out[...] = states_ref[...]
    weight_out[...] = weight_ref[...]
    row = lax.broadcasted_iota(jnp.int32, first_ref.shape, 0)
    first = jnp.zeros(first_ref.shape, jnp.int32)
    end = jnp.zeros(first_ref.shape, jnp.int32)
    base = base_ref[0]
    for patch in range(patches):
        begin = starts_ref[patch] - base
        first = jnp.where(row == patch, begin, first)
        if patch > 0:
            end = jnp.where(row == patch - 1, begin, end)
    first_ref[...] = first
    end_ref[...] = jnp.where(row == patches - 1, shard_bytes + straddle_ref[0], end)


def own_keys(base, starts, straddle, states, key_weight):
    patches = starts.shape[0]
    bounds = jax.ShapeDtypeStruct((patches, 128), jnp.int32)
    return pl.pallas_call(
        keys_kernel,
        out_shape=(
            jax.ShapeDtypeStruct(states.shape, jnp.bfloat16),
            bounds,
            bounds,
            jax.ShapeDtypeStruct(states.shape, jnp.bfloat16),
            jax.ShapeDtypeStruct(key_weight.shape, jnp.bfloat16),
        ),
        in_specs=scalars(3) + whole(2),
        out_specs=tuple(whole(5)),
        compiler_params=pltpu.CompilerParams(vmem_limit_bytes=8 << 20),
        name="own_keys",
    )(base.reshape(1), starts, straddle, states, key_weight)


def pool_kernel(first_ref, end_ref, states_ref, halo_ref, keys_ref, weight_ref, out_ref):
    window = jnp.concatenate([states_ref[...], halo_ref[...]], axis=0)
    halo_keys = jnp.dot(
        halo_ref[...], weight_ref[...], preferred_element_type=jnp.float32
    ).astype(jnp.bfloat16)
    keys = jnp.concatenate([keys_ref[...], halo_keys], axis=0)
    patches = first_ref.shape[0]
    position = lax.broadcasted_iota(jnp.int32, (patches, window.shape[0]), 1)
    member = (position >= first_ref[:, :1]) & (position < end_ref[:, :1])
    ones = jnp.where(member, jnp.float32(1.0), jnp.float32(0.0))
    byte_count = jnp.sum(ones, axis=1, keepdims=True)
    query = (
        jnp.dot(ones.astype(jnp.bfloat16), window, preferred_element_type=jnp.float32) / byte_count
    ).astype(jnp.bfloat16)
    pooled = []
    for head in range(window.shape[1] // LHD):
        part = slice(head * LHD, (head + 1) * LHD)
        scores = lax.dot_general(
            query[:, part],
            keys[:, part],
            (((1,), (1,)), ((), ())),
            preferred_element_type=jnp.float32,
        ) * jnp.float32(LHD**-0.5)
        scores = jnp.where(member, scores, jnp.float32(-1e30))
        row_peak = jnp.max(scores, axis=1, keepdims=True)
        expo = jnp.where(member, jnp.exp(scores - row_peak), jnp.float32(0.0))
        cross = (expo / jnp.sum(expo, axis=1, keepdims=True)).astype(jnp.bfloat16)
        pooled.append(
            jnp.dot(cross, window[:, part], preferred_element_type=jnp.float32).astype(jnp.bfloat16)
        )
    block = jnp.concatenate(pooled, axis=1)
    for target in range(out_ref.shape[0]):
        out_ref[target] = block


def pool(first, end, states, halo, keys, key_weight, copies):
    patches, width = first.shape[0], states.shape[1]
    return pl.pallas_call(
        pool_kernel,
        out_shape=jax.ShapeDtypeStruct((copies, patches, width), jnp.bfloat16),
        in_specs=whole(6),
        out_specs=pl.BlockSpec(memory_space=pltpu.VMEM),
        compiler_params=pltpu.CompilerParams(vmem_limit_bytes=16 << 20),
        name="pool",
    )(first, end, states, halo, keys, key_weight)


def merge_kernel(blocks_ref, weight_ref, out_ref, total_ref):
    step = pl.program_id(0)

    @pl.when(step == 0)
    def _():
        total_ref[...] = jnp.zeros_like(total_ref)

    high, low = [], []
    for shard in range(blocks_ref.shape[0]):
        gain = blocks_ref[shard, ROWS:, :].astype(jnp.float32)[:1]
        scaled = blocks_ref[shard, :ROWS, :].astype(jnp.float32) * gain
        top = scaled.astype(jnp.bfloat16)
        high.append(top)
        low.append((scaled - top.astype(jnp.float32)).astype(jnp.bfloat16))
    both = jnp.concatenate(
        [jnp.concatenate(high, axis=1), jnp.concatenate(low, axis=1)], axis=0
    )
    for part in range(weight_ref.shape[0]):
        total_ref[:, part * HD : (part + 1) * HD] += jnp.dot(
            both, weight_ref[part], preferred_element_type=jnp.float32
        )

    @pl.when(step == pl.num_programs(0) - 1)
    def _():
        out_ref[...] = (total_ref[:ROWS] + total_ref[ROWS:]).astype(jnp.bfloat16)


def merge_weights(blocks, attn_weight):
    shards_total, block_rows, columns = blocks.shape
    steps = 4
    group = shards_total // steps
    planes = jnp.swapaxes(attn_weight, 0, 1)
    parts, _, width = planes.shape
    return pl.pallas_call(
        merge_kernel,
        out_shape=jax.ShapeDtypeStruct((ROWS, parts * width), jnp.bfloat16),
        grid=(steps,),
        in_specs=[
            pl.BlockSpec((group, block_rows, columns), lambda s: (s, 0, 0)),
            pl.BlockSpec((parts, group * columns, width), lambda s: (0, s, 0)),
        ],
        out_specs=pl.BlockSpec((ROWS, parts * width), lambda s: (0, 0)),
        scratch_shapes=[pltpu.VMEM((2 * ROWS, parts * width), jnp.float32)],
        compiler_params=pltpu.CompilerParams(vmem_limit_bytes=16 << 20),
        name="merge",
    )(blocks, planes)


def attend_kernel(model_width, square_ref, pooled_ref, merged_ref, out_ref, view_ref):
    square = jnp.sum(square_ref[...], axis=0) / jnp.float32(model_width)
    inverse = lax.rsqrt(square + jnp.float32(epsilon))
    diagonal = lax.broadcasted_iota(jnp.int32, (128, 128), 0) == lax.broadcasted_iota(
        jnp.int32, (128, 128), 1
    )
    patches = pooled_ref.shape[0]
    for tile in range(patches // 128):
        rows = slice(tile * 128, (tile + 1) * 128)
        spread_row = jnp.broadcast_to(inverse[tile : tile + 1, :], (128, 128))
        column = jnp.sum(
            jnp.where(diagonal, spread_row, jnp.float32(0.0)), axis=1, keepdims=True
        )
        view_ref[rows, :] = (
            jnp.dot(pooled_ref[rows, :], merged_ref[...], preferred_element_type=jnp.float32)
            * column
        ).astype(jnp.bfloat16)
    for tile in range(patches // TILE):
        rows = slice(tile * TILE, (tile + 1) * TILE)
        seen = (tile + 1) * TILE
        scores = lax.dot_general(
            view_ref[rows, :HD],
            view_ref[:seen, HD : 2 * HD],
            (((1,), (1,)), ((), ())),
            preferred_element_type=jnp.float32,
        ) * jnp.float32(HD**-0.5)
        causal = lax.broadcasted_iota(jnp.int32, (TILE, seen), 0) + tile * TILE >= (
            lax.broadcasted_iota(jnp.int32, (TILE, seen), 1)
        )
        scores = jnp.where(causal, scores, jnp.float32(-1e30))
        row_peak = jnp.max(scores, axis=1, keepdims=True)
        expo = jnp.exp(scores - row_peak)
        probs = (expo * (jnp.float32(1.0) / jnp.sum(expo, axis=1, keepdims=True))).astype(
            jnp.bfloat16
        )
        out_ref[rows, :] = jnp.dot(
            probs, view_ref[:seen, 2 * HD :], preferred_element_type=jnp.float32
        ).astype(jnp.bfloat16)


def attend(model_width, square_all, pooled_all, merged_all):
    patches = pooled_all.shape[0]
    return pl.pallas_call(
        functools.partial(attend_kernel, model_width),
        out_shape=jax.ShapeDtypeStruct((patches, HD), jnp.bfloat16),
        in_specs=whole(3),
        out_specs=pl.BlockSpec(memory_space=pltpu.VMEM),
        scratch_shapes=[pltpu.VMEM((patches, merged_all.shape[1]), jnp.bfloat16)],
        compiler_params=pltpu.CompilerParams(vmem_limit_bytes=24 << 20),
        name="attend",
    )(square_all, pooled_all, merged_all)


def exchange(blocks, axis):
    return lax.all_to_all(blocks, axis, split_axis=0, concat_axis=0, tiled=True)


def layer(states, starts, straddle, key_weight, out_weight, norm_gain, attn_weight):
    seq = lax.axis_size("seq")
    base = lax.axis_index("seq") * states.shape[0]
    model_width = attn_weight.shape[0]
    pooled_width = out_weight.shape[0]

    weight_blocks = exchange(weight_rows(out_weight, norm_gain, lax.axis_index("rep"), seq), "seq")
    halo_rows = shifted(states[:HALO], "seq", -1)
    keys, first, end, own, weight = own_keys(base, starts, straddle, states, key_weight)
    pooled_blocks = pool(first, end, own, halo_rows, keys, weight, seq)
    pooled_all = exchange(pooled_blocks, "seq").reshape(-1, pooled_width)
    merged = merge_weights(weight_blocks, attn_weight)
    merged_all = lax.all_gather(merged, "rep", axis=0, tiled=True)
    part = lax.dot_general(
        out_weight, pooled_all, (((0,), (1,)), ((), ())), preferred_element_type=jnp.float32
    )
    part_square = jnp.sum(part * part, axis=0).reshape(-1, 128)
    square_all = exchange(jnp.broadcast_to(part_square[None], (seq,) + part_square.shape), "seq")
    attended = attend(model_width, square_all, pooled_all, merged_all)
    return lax.all_to_all(attended, "seq", split_axis=0, concat_axis=1, tiled=True)


def solution(mesh):
    placed = (
        P(("rep", "seq"), None),
        P(("rep", "seq")),
        P(("rep", "seq")),
        P(),
        P(None, "seq"),
        P("seq"),
        P(None, None, "seq"),
    )
    return jax.shard_map(
        layer, mesh=mesh, in_specs=placed, out_specs=P(("rep", "seq"), None), check_vma=False
    )
```

```python
import functools

import jax
import jax.numpy as jnp
from jax import lax
from jax.experimental import pallas as pl
from jax.experimental.pallas import tpu as pltpu
from jax.sharding import PartitionSpec as P


HD = 128
LHD = 128
HALO = 64
ROWS = 32
TILE = 256
WIDE = 512


epsilon = 1e-05


def shifted(shard, axis, by):
    size = lax.axis_size(axis)
    pairs = [(i, i + by) for i in range(size) if 0 <= i + by < size]
    return lax.ppermute(shard, axis, pairs)


def whole(count):
    return [pl.BlockSpec(memory_space=pltpu.VMEM)] * count


def scalars(count):
    return [pl.BlockSpec(memory_space=pltpu.SMEM)] * count


def prepare_kernel(
    index_ref, base_ref, starts_ref, straddle_ref, out_weight_ref, gain_ref, states_ref, weight_ref,
    blocks_ref, halo_ref, keys_ref, first_ref, end_ref, own_ref, own_weight_ref,
    rows_ref, columns_ref, sems,
):
    start = pl.multiple_of(index_ref[0] * ROWS, ROWS)
    copies = [
        pltpu.make_async_copy(out_weight_ref.at[pl.ds(start, ROWS), :], rows_ref, sems.at[0]),
        pltpu.make_async_copy(gain_ref, columns_ref, sems.at[1]),
        pltpu.make_async_copy(states_ref, own_ref, sems.at[2]),
        pltpu.make_async_copy(weight_ref, own_weight_ref, sems.at[3]),
    ]
    for copy in copies:
        copy.start()
    patches = first_ref.shape[0]
    row = lax.broadcasted_iota(jnp.int32, first_ref.shape, 0)
    first = jnp.zeros(first_ref.shape, jnp.int32)
    end = jnp.zeros(first_ref.shape, jnp.int32)
    base = base_ref[0]
    for patch in range(patches):
        begin = starts_ref[patch] - base
        first = jnp.where(row == patch, begin, first)
        if patch > 0:
            end = jnp.where(row == patch - 1, begin, end)
    first_ref[...] = first
    end_ref[...] = jnp.where(row == patches - 1, own_ref.shape[0] + straddle_ref[0], end)
    copies[0].wait()
    copies[1].wait()
    block = (
        rows_ref[...].astype(jnp.float32) * columns_ref[...].astype(jnp.float32)
    ).astype(jnp.bfloat16)
    for target in range(blocks_ref.shape[0]):
        blocks_ref[target] = block
    copies[2].wait()
    halo_ref[...] = own_ref[:HALO, :]
    copies[3].wait()
    keys_ref[...] = jnp.dot(
        own_ref[...], own_weight_ref[...], preferred_element_type=jnp.float32
    ).astype(jnp.bfloat16)


def prepare(index, base, starts, straddle, out_weight, norm_gain, states, key_weight, copies):
    patches, width = starts.shape[0], states.shape[1]
    columns = out_weight.shape[1]
    bounds = jax.ShapeDtypeStruct((patches, 128), jnp.int32)
    return pl.pallas_call(
        prepare_kernel,
        out_shape=(
            jax.ShapeDtypeStruct((copies, ROWS, columns), jnp.bfloat16),
            jax.ShapeDtypeStruct((HALO, width), jnp.bfloat16),
            jax.ShapeDtypeStruct(states.shape, jnp.bfloat16),
            bounds,
            bounds,
            jax.ShapeDtypeStruct(states.shape, jnp.bfloat16),
            jax.ShapeDtypeStruct(key_weight.shape, jnp.bfloat16),
        ),
        in_specs=scalars(4) + [pl.BlockSpec(memory_space=pltpu.HBM)] * 4,
        out_specs=tuple(whole(7)),
        scratch_shapes=[
            pltpu.VMEM((ROWS, columns), jnp.bfloat16),
            pltpu.VMEM((1, columns), jnp.bfloat16),
            pltpu.SemaphoreType.DMA((4,)),
        ],
        name="prepare",
    )(
        index.reshape(1), base.reshape(1), starts, straddle,
        out_weight, norm_gain.reshape(1, -1), states, key_weight,
    )


def pool_kernel(first_ref, end_ref, states_ref, halo_ref, keys_ref, weight_ref, out_ref):
    window = jnp.concatenate([states_ref[...], halo_ref[...]], axis=0)
    halo_keys = jnp.dot(
        halo_ref[...], weight_ref[...], preferred_element_type=jnp.float32
    ).astype(jnp.bfloat16)
    keys = jnp.concatenate([keys_ref[...], halo_keys], axis=0)
    patches = first_ref.shape[0]
    position = lax.broadcasted_iota(jnp.int32, (patches, window.shape[0]), 1)
    member = (position >= first_ref[:, :1]) & (position < end_ref[:, :1])
    ones = jnp.where(member, jnp.float32(1.0), jnp.float32(0.0))
    byte_count = jnp.sum(ones, axis=1, keepdims=True)
    query = (
        jnp.dot(ones.astype(jnp.bfloat16), window, preferred_element_type=jnp.float32) / byte_count
    ).astype(jnp.bfloat16)
    pooled = []
    for head in range(window.shape[1] // LHD):
        part = slice(head * LHD, (head + 1) * LHD)
        scores = lax.dot_general(
            query[:, part],
            keys[:, part],
            (((1,), (1,)), ((), ())),
            preferred_element_type=jnp.float32,
        ) * jnp.float32(LHD**-0.5)
        scores = jnp.where(member, scores, jnp.float32(-1e30))
        row_peak = jnp.max(scores, axis=1, keepdims=True)
        expo = jnp.where(member, jnp.exp(scores - row_peak), jnp.float32(0.0))
        cross = (expo / jnp.sum(expo, axis=1, keepdims=True)).astype(jnp.bfloat16)
        pooled.append(
            jnp.dot(cross, window[:, part], preferred_element_type=jnp.float32).astype(jnp.bfloat16)
        )
    block = jnp.concatenate(pooled, axis=1)
    for target in range(out_ref.shape[0]):
        out_ref[target] = block


def pool(first, end, states, halo, keys, key_weight, copies):
    patches, width = first.shape[0], states.shape[1]
    return pl.pallas_call(
        pool_kernel,
        out_shape=jax.ShapeDtypeStruct((copies, patches, width), jnp.bfloat16),
        in_specs=whole(6),
        out_specs=pl.BlockSpec(memory_space=pltpu.VMEM),
        name="pool",
    )(first, end, states, halo, keys, key_weight)


def merge_kernel(blocks_ref, weight_ref, out_ref, total_ref):
    step = pl.program_id(0)

    @pl.when(step == 0)
    def _():
        total_ref[...] = jnp.zeros_like(total_ref)

    rows = jnp.concatenate([blocks_ref[shard] for shard in range(blocks_ref.shape[0])], axis=1)
    for part in range(weight_ref.shape[0]):
        total_ref[:, part * HD : (part + 1) * HD] += jnp.dot(
            rows, weight_ref[part], preferred_element_type=jnp.float32
        )

    @pl.when(step == pl.num_programs(0) - 1)
    def _():
        out_ref[...] = total_ref[...].astype(jnp.bfloat16)


def merge_weights(blocks, attn_weight):
    shards_total, block_rows, columns = blocks.shape
    steps = 4
    group = shards_total // steps
    planes = jnp.swapaxes(attn_weight, 0, 1)
    parts, _, width = planes.shape
    return pl.pallas_call(
        merge_kernel,
        out_shape=jax.ShapeDtypeStruct((ROWS, parts * width), jnp.bfloat16),
        grid=(steps,),
        in_specs=[
            pl.BlockSpec((group, block_rows, columns), lambda s: (s, 0, 0)),
            pl.BlockSpec((parts, group * columns, width), lambda s: (0, s, 0)),
        ],
        out_specs=pl.BlockSpec((ROWS, parts * width), lambda s: (0, 0)),
        scratch_shapes=[pltpu.VMEM((ROWS, parts * width), jnp.float32)],
        compiler_params=pltpu.CompilerParams(vmem_limit_bytes=16 << 20),
        name="merge",
    )(blocks, planes)


def attend_kernel(model_width, square_ref, pooled_ref, merged_ref, out_ref, view_ref):
    square = jnp.sum(square_ref[...], axis=0) / jnp.float32(model_width)
    inverse = lax.rsqrt(square + jnp.float32(epsilon))
    diagonal = lax.broadcasted_iota(jnp.int32, (128, 128), 0) == lax.broadcasted_iota(
        jnp.int32, (128, 128), 1
    )
    patches = pooled_ref.shape[0]
    columns = []
    for tile in range(patches // 128):
        spread_row = jnp.broadcast_to(inverse[tile : tile + 1, :], (128, 128))
        columns.append(
            jnp.sum(jnp.where(diagonal, spread_row, jnp.float32(0.0)), axis=1, keepdims=True)
        )
    for tile in range(patches // WIDE):
        rows = slice(tile * WIDE, (tile + 1) * WIDE)
        column = jnp.concatenate(columns[tile * WIDE // 128 : (tile + 1) * WIDE // 128], axis=0)
        view_ref[rows, :] = (
            jnp.dot(pooled_ref[rows, :], merged_ref[...], preferred_element_type=jnp.float32)
            * column
        ).astype(jnp.bfloat16)
    causal = lax.broadcasted_iota(jnp.int32, (TILE, TILE), 0) >= lax.broadcasted_iota(
        jnp.int32, (TILE, TILE), 1
    )
    scale = jnp.float32(HD**-0.5)
    for tile in range(patches // TILE):
        rows = slice(tile * TILE, (tile + 1) * TILE)
        query = view_ref[rows, :HD]

        def against(keys):
            return lax.dot_general(
                query, keys, (((1,), (1,)), ((), ())), preferred_element_type=jnp.float32
            )

        near = jnp.where(causal, against(view_ref[rows, HD : 2 * HD]), jnp.float32(-1e30))
        peak = jnp.max(near, axis=1, keepdims=True)
        if tile > 0:
            far = against(view_ref[: tile * TILE, HD : 2 * HD])
            peak = jnp.maximum(peak, jnp.max(far, axis=1, keepdims=True))
        near = jnp.exp((near - peak) * scale)
        total = jnp.sum(near, axis=1, keepdims=True)
        result = jnp.dot(
            near.astype(jnp.bfloat16), view_ref[rows, 2 * HD :], preferred_element_type=jnp.float32
        )
        if tile > 0:
            far = jnp.exp((far - peak) * scale)
            total = total + jnp.sum(far, axis=1, keepdims=True)
            result = result + jnp.dot(
                far.astype(jnp.bfloat16),
                view_ref[: tile * TILE, 2 * HD :],
                preferred_element_type=jnp.float32,
            )
        out_ref[rows, :] = (result * (jnp.float32(1.0) / total)).astype(jnp.bfloat16)


def attend(model_width, square_all, pooled_all, merged_all):
    patches = pooled_all.shape[0]
    return pl.pallas_call(
        functools.partial(attend_kernel, model_width),
        out_shape=jax.ShapeDtypeStruct((patches, HD), jnp.bfloat16),
        in_specs=whole(3),
        out_specs=pl.BlockSpec(memory_space=pltpu.VMEM),
        scratch_shapes=[pltpu.VMEM((patches, merged_all.shape[1]), jnp.bfloat16)],
        compiler_params=pltpu.CompilerParams(vmem_limit_bytes=24 << 20),
        name="attend",
    )(square_all, pooled_all, merged_all)


def exchange(blocks, axis):
    return lax.all_to_all(blocks, axis, split_axis=0, concat_axis=0, tiled=True)


def layer(states, starts, straddle, key_weight, out_weight, norm_gain, attn_weight):
    seq = lax.axis_size("seq")
    base = lax.axis_index("seq") * states.shape[0]
    model_width = attn_weight.shape[0]
    pooled_width = out_weight.shape[0]

    row_blocks, edge, keys, first, end, own, weight = prepare(
        lax.axis_index("rep"), base, starts, straddle,
        out_weight, norm_gain, states, key_weight, seq,
    )
    weight_blocks = exchange(row_blocks, "seq")
    halo_rows = shifted(edge, "seq", -1)
    pooled_blocks = pool(first, end, own, halo_rows, keys, weight, seq)
    pooled_all = exchange(pooled_blocks, "seq").reshape(-1, pooled_width)
    merged = merge_weights(weight_blocks, attn_weight)
    merged_all = lax.all_gather(merged, "rep", axis=0, tiled=True)
    part = lax.dot_general(
        out_weight, pooled_all, (((0,), (1,)), ((), ())), preferred_element_type=jnp.float32
    )
    part_square = jnp.sum(part * part, axis=0).reshape(-1, 128)
    square_all = exchange(jnp.broadcast_to(part_square[None], (seq,) + part_square.shape), "seq")
    attended = attend(model_width, square_all, pooled_all, merged_all)
    return lax.all_to_all(attended, "seq", split_axis=0, concat_axis=1, tiled=True)


def solution(mesh):
    placed = (
        P(("rep", "seq"), None),
        P(("rep", "seq")),
        P(("rep", "seq")),
        P(),
        P(None, "seq"),
        P("seq"),
        P(None, None, "seq"),
    )
    return jax.shard_map(
        layer, mesh=mesh, in_specs=placed, out_specs=P(("rep", "seq"), None), check_vma=False
    )
```

```python
import functools

import jax
import jax.numpy as jnp
from jax import lax
from jax.experimental import pallas as pl
from jax.experimental.pallas import tpu as pltpu
from jax.sharding import PartitionSpec as P


HD = 128
LHD = 128
HALO = 64
ROWS = 32
TILE = 256
WIDE = 512


epsilon = 1e-05


def shifted(shard, axis, by):
    size = lax.axis_size(axis)
    pairs = [(i, i + by) for i in range(size) if 0 <= i + by < size]
    return lax.ppermute(shard, axis, pairs)


def whole(count):
    return [pl.BlockSpec(memory_space=pltpu.VMEM)] * count


def scalars(count):
    return [pl.BlockSpec(memory_space=pltpu.SMEM)] * count


def rows_kernel(index_ref, weight_ref, gain_ref, states_ref, out_ref, edge_ref):
    block = (weight_ref[...].astype(jnp.float32) * gain_ref[...].astype(jnp.float32)).astype(
        jnp.bfloat16
    )
    for target in range(out_ref.shape[0]):
        out_ref[target] = block
    edge_ref[...] = states_ref[...]


def weight_rows(out_weight, norm_gain, states, index, copies):
    columns, width = out_weight.shape[1], states.shape[1]
    return pl.pallas_call(
        rows_kernel,
        out_shape=(
            jax.ShapeDtypeStruct((copies, ROWS, columns), jnp.bfloat16),
            jax.ShapeDtypeStruct((HALO, width), jnp.bfloat16),
        ),
        grid_spec=pltpu.PrefetchScalarGridSpec(
            num_scalar_prefetch=1,
            grid=(1,),
            in_specs=[
                pl.BlockSpec((ROWS, columns), lambda step, index: (index[0], 0)),
                pl.BlockSpec((1, columns), lambda step, index: (0, 0)),
                pl.BlockSpec((HALO, width), lambda step, index: (0, 0)),
            ],
            out_specs=[
                pl.BlockSpec((copies, ROWS, columns), lambda step, index: (0, 0, 0)),
                pl.BlockSpec((HALO, width), lambda step, index: (0, 0)),
            ],
        ),
        name="rows",
    )(index.reshape(1), out_weight, norm_gain.reshape(1, -1), states)


def keys_kernel(base_ref, starts_ref, straddle_ref, states_ref, weight_ref, keys_ref, first_ref, end_ref, states_out, weight_out):
    patches = first_ref.shape[0]
    shard_bytes = states_ref.shape[0]
    keys_ref[...] = jnp.dot(
        states_ref[...], weight_ref[...], preferred_element_type=jnp.float32
    ).astype(jnp.bfloat16)
    states_out[...] = states_ref[...]
    weight_out[...] = weight_ref[...]
    row = lax.broadcasted_iota(jnp.int32, first_ref.shape, 0)
    first = jnp.zeros(first_ref.shape, jnp.int32)
    end = jnp.zeros(first_ref.shape, jnp.int32)
    base = base_ref[0]
    for patch in range(patches):
        begin = starts_ref[patch] - base
        first = jnp.where(row == patch, begin, first)
        if patch > 0:
            end = jnp.where(row == patch - 1, begin, end)
    first_ref[...] = first
    end_ref[...] = jnp.where(row == patches - 1, shard_bytes + straddle_ref[0], end)


def own_keys(base, starts, straddle, states, key_weight):
    patches = starts.shape[0]
    bounds = jax.ShapeDtypeStruct((patches, 128), jnp.int32)
    return pl.pallas_call(
        keys_kernel,
        out_shape=(
            jax.ShapeDtypeStruct(states.shape, jnp.bfloat16),
            bounds,
            bounds,
            jax.ShapeDtypeStruct(states.shape, jnp.bfloat16),
            jax.ShapeDtypeStruct(key_weight.shape, jnp.bfloat16),
        ),
        in_specs=scalars(3) + whole(2),
        out_specs=tuple(whole(5)),
        compiler_params=pltpu.CompilerParams(vmem_limit_bytes=8 << 20),
        name="own_keys",
    )(base.reshape(1), starts, straddle, states, key_weight)


def pool_kernel(first_ref, end_ref, states_ref, halo_ref, keys_ref, weight_ref, out_ref):
    window = jnp.concatenate([states_ref[...], halo_ref[...]], axis=0)
    halo_keys = jnp.dot(
        halo_ref[...], weight_ref[...], preferred_element_type=jnp.float32
    ).astype(jnp.bfloat16)
    keys = jnp.concatenate([keys_ref[...], halo_keys], axis=0)
    patches = first_ref.shape[0]
    position = lax.broadcasted_iota(jnp.int32, (patches, window.shape[0]), 1)
    member = (position >= first_ref[:, :1]) & (position < end_ref[:, :1])
    ones = jnp.where(member, jnp.float32(1.0), jnp.float32(0.0))
    byte_count = jnp.sum(ones, axis=1, keepdims=True)
    query = (
        jnp.dot(ones.astype(jnp.bfloat16), window, preferred_element_type=jnp.float32) / byte_count
    ).astype(jnp.bfloat16)
    pooled = []
    for head in range(window.shape[1] // LHD):
        part = slice(head * LHD, (head + 1) * LHD)
        scores = lax.dot_general(
            query[:, part],
            keys[:, part],
            (((1,), (1,)), ((), ())),
            preferred_element_type=jnp.float32,
        ) * jnp.float32(LHD**-0.5)
        scores = jnp.where(member, scores, jnp.float32(-1e30))
        row_peak = jnp.max(scores, axis=1, keepdims=True)
        expo = jnp.where(member, jnp.exp(scores - row_peak), jnp.float32(0.0))
        cross = (expo / jnp.sum(expo, axis=1, keepdims=True)).astype(jnp.bfloat16)
        pooled.append(
            jnp.dot(cross, window[:, part], preferred_element_type=jnp.float32).astype(jnp.bfloat16)
        )
    block = jnp.concatenate(pooled, axis=1)
    for target in range(out_ref.shape[0]):
        out_ref[target] = block


def pool(first, end, states, halo, keys, key_weight, copies):
    patches, width = first.shape[0], states.shape[1]
    return pl.pallas_call(
        pool_kernel,
        out_shape=jax.ShapeDtypeStruct((copies, patches, width), jnp.bfloat16),
        in_specs=whole(6),
        out_specs=pl.BlockSpec(memory_space=pltpu.VMEM),
        compiler_params=pltpu.CompilerParams(vmem_limit_bytes=16 << 20),
        name="pool",
    )(first, end, states, halo, keys, key_weight)


def merge_kernel(blocks_ref, weight_ref, out_ref, total_ref):
    step = pl.program_id(0)

    @pl.when(step == 0)
    def _():
        total_ref[...] = jnp.zeros_like(total_ref)

    rows = jnp.concatenate([blocks_ref[shard] for shard in range(blocks_ref.shape[0])], axis=1)
    for part in range(weight_ref.shape[0]):
        total_ref[:, part * HD : (part + 1) * HD] += jnp.dot(
            rows, weight_ref[part], preferred_element_type=jnp.float32
        )

    @pl.when(step == pl.num_programs(0) - 1)
    def _():
        out_ref[...] = total_ref[...].astype(jnp.bfloat16)


def merge_weights(blocks, attn_weight):
    shards_total, block_rows, columns = blocks.shape
    steps = 4
    group = shards_total // steps
    planes = jnp.swapaxes(attn_weight, 0, 1)
    parts, _, width = planes.shape
    return pl.pallas_call(
        merge_kernel,
        out_shape=jax.ShapeDtypeStruct((ROWS, parts * width), jnp.bfloat16),
        grid=(steps,),
        in_specs=[
            pl.BlockSpec((group, block_rows, columns), lambda s: (s, 0, 0)),
            pl.BlockSpec((parts, group * columns, width), lambda s: (0, s, 0)),
        ],
        out_specs=pl.BlockSpec((ROWS, parts * width), lambda s: (0, 0)),
        scratch_shapes=[pltpu.VMEM((ROWS, parts * width), jnp.float32)],
        compiler_params=pltpu.CompilerParams(vmem_limit_bytes=16 << 20),
        name="merge",
    )(blocks, planes)


def attend_kernel(model_width, square_ref, pooled_ref, merged_ref, out_ref, view_ref):
    square = jnp.sum(square_ref[...], axis=0) / jnp.float32(model_width)
    inverse = lax.rsqrt(square + jnp.float32(epsilon))
    diagonal = lax.broadcasted_iota(jnp.int32, (128, 128), 0) == lax.broadcasted_iota(
        jnp.int32, (128, 128), 1
    )
    patches = pooled_ref.shape[0]
    columns = []
    for tile in range(patches // 128):
        spread_row = jnp.broadcast_to(inverse[tile : tile + 1, :], (128, 128))
        columns.append(
            jnp.sum(jnp.where(diagonal, spread_row, jnp.float32(0.0)), axis=1, keepdims=True)
        )
    for tile in range(patches // WIDE):
        rows = slice(tile * WIDE, (tile + 1) * WIDE)
        column = jnp.concatenate(columns[tile * WIDE // 128 : (tile + 1) * WIDE // 128], axis=0)
        view_ref[rows, :] = (
            jnp.dot(pooled_ref[rows, :], merged_ref[...], preferred_element_type=jnp.float32)
            * column
        ).astype(jnp.bfloat16)
    causal = lax.broadcasted_iota(jnp.int32, (TILE, TILE), 0) >= lax.broadcasted_iota(
        jnp.int32, (TILE, TILE), 1
    )
    scale = jnp.float32(HD**-0.5)
    for tile in range(patches // TILE):
        rows = slice(tile * TILE, (tile + 1) * TILE)
        query = view_ref[rows, :HD]

        def against(keys):
            return lax.dot_general(
                query, keys, (((1,), (1,)), ((), ())), preferred_element_type=jnp.float32
            )

        near = jnp.where(causal, against(view_ref[rows, HD : 2 * HD]), jnp.float32(-1e30))
        peak = jnp.max(near, axis=1, keepdims=True)
        if tile > 0:
            far = against(view_ref[: tile * TILE, HD : 2 * HD])
            peak = jnp.maximum(peak, jnp.max(far, axis=1, keepdims=True))
        near = jnp.exp((near - peak) * scale)
        total = jnp.sum(near, axis=1, keepdims=True)
        result = jnp.dot(
            near.astype(jnp.bfloat16), view_ref[rows, 2 * HD :], preferred_element_type=jnp.float32
        )
        if tile > 0:
            far = jnp.exp((far - peak) * scale)
            total = total + jnp.sum(far, axis=1, keepdims=True)
            result = result + jnp.dot(
                far.astype(jnp.bfloat16),
                view_ref[: tile * TILE, 2 * HD :],
                preferred_element_type=jnp.float32,
            )
        out_ref[rows, :] = (result * (jnp.float32(1.0) / total)).astype(jnp.bfloat16)


def attend(model_width, square_all, pooled_all, merged_all):
    patches = pooled_all.shape[0]
    return pl.pallas_call(
        functools.partial(attend_kernel, model_width),
        out_shape=jax.ShapeDtypeStruct((patches, HD), jnp.bfloat16),
        in_specs=whole(3),
        out_specs=pl.BlockSpec(memory_space=pltpu.VMEM),
        scratch_shapes=[pltpu.VMEM((patches, merged_all.shape[1]), jnp.bfloat16)],
        compiler_params=pltpu.CompilerParams(vmem_limit_bytes=24 << 20),
        name="attend",
    )(square_all, pooled_all, merged_all)


def exchange(blocks, axis):
    return lax.all_to_all(blocks, axis, split_axis=0, concat_axis=0, tiled=True)


def layer(states, starts, straddle, key_weight, out_weight, norm_gain, attn_weight):
    seq = lax.axis_size("seq")
    base = lax.axis_index("seq") * states.shape[0]
    model_width = attn_weight.shape[0]
    pooled_width = out_weight.shape[0]

    row_blocks, edge = weight_rows(out_weight, norm_gain, states, lax.axis_index("rep"), seq)
    weight_blocks = exchange(row_blocks, "seq")
    halo_rows = shifted(edge, "seq", -1)
    keys, first, end, own, weight = own_keys(base, starts, straddle, states, key_weight)
    pooled_blocks = pool(first, end, own, halo_rows, keys, weight, seq)
    pooled_all = exchange(pooled_blocks, "seq").reshape(-1, pooled_width)
    merged = merge_weights(weight_blocks, attn_weight)
    merged_all = lax.all_gather(merged, "rep", axis=0, tiled=True)
    part = lax.dot_general(
        out_weight, pooled_all, (((0,), (1,)), ((), ())), preferred_element_type=jnp.float32
    )
    part_square = jnp.sum(part * part, axis=0).reshape(-1, 128)
    square_all = exchange(jnp.broadcast_to(part_square[None], (seq,) + part_square.shape), "seq")
    attended = attend(model_width, square_all, pooled_all, merged_all)
    return lax.all_to_all(attended, "seq", split_axis=0, concat_axis=1, tiled=True)


def solution(mesh):
    placed = (
        P(("rep", "seq"), None),
        P(("rep", "seq")),
        P(("rep", "seq")),
        P(),
        P(None, "seq"),
        P("seq"),
        P(None, None, "seq"),
    )
    return jax.shard_map(
        layer, mesh=mesh, in_specs=placed, out_specs=P(("rep", "seq"), None), check_vma=False
    )
```

```python
import functools

import jax
import jax.numpy as jnp
from jax import lax
from jax.experimental import pallas as pl
from jax.experimental.pallas import tpu as pltpu
from jax.sharding import PartitionSpec as P


HD = 128
LHD = 128
HALO = 64
ROWS = 32
ALONG_X = 4
TILE = 256
WIDE = 512


epsilon = 1e-05


def shifted(shard, axis, by):
    size = lax.axis_size(axis)
    pairs = [(i, i + by) for i in range(size) if 0 <= i + by < size]
    return lax.ppermute(shard, axis, pairs)


def whole(count):
    return [pl.BlockSpec(memory_space=pltpu.VMEM)] * count


def scalars(count):
    return [pl.BlockSpec(memory_space=pltpu.SMEM)] * count


def rows_kernel(index_ref, weight_ref, gain_ref, states_ref, out_ref, edge_ref):
    block = (weight_ref[...].astype(jnp.float32) * gain_ref[...].astype(jnp.float32)).astype(
        jnp.bfloat16
    )
    for target in range(out_ref.shape[0]):
        out_ref[target] = block
    edge_ref[...] = states_ref[...]


def weight_rows(out_weight, norm_gain, states, index, copies):
    columns, width = out_weight.shape[1], states.shape[1]
    return pl.pallas_call(
        rows_kernel,
        out_shape=(
            jax.ShapeDtypeStruct((copies, ROWS, columns), jnp.bfloat16),
            jax.ShapeDtypeStruct((HALO, width), jnp.bfloat16),
        ),
        grid_spec=pltpu.PrefetchScalarGridSpec(
            num_scalar_prefetch=1,
            grid=(1,),
            in_specs=[
                pl.BlockSpec((ROWS, columns), lambda step, index: (index[0], 0)),
                pl.BlockSpec((1, columns), lambda step, index: (0, 0)),
                pl.BlockSpec((HALO, width), lambda step, index: (0, 0)),
            ],
            out_specs=[
                pl.BlockSpec((copies, ROWS, columns), lambda step, index: (0, 0, 0)),
                pl.BlockSpec((HALO, width), lambda step, index: (0, 0)),
            ],
        ),
        name="rows",
    )(index.reshape(1), out_weight, norm_gain.reshape(1, -1), states)


def keys_kernel(base_ref, starts_ref, straddle_ref, states_ref, weight_ref, keys_ref, first_ref, end_ref, states_out, weight_out):
    patches = first_ref.shape[0]
    shard_bytes = states_ref.shape[0]
    keys_ref[...] = jnp.dot(
        states_ref[...], weight_ref[...], preferred_element_type=jnp.float32
    ).astype(jnp.bfloat16)
    states_out[...] = states_ref[...]
    weight_out[...] = weight_ref[...]
    row = lax.broadcasted_iota(jnp.int32, first_ref.shape, 0)
    first = jnp.zeros(first_ref.shape, jnp.int32)
    end = jnp.zeros(first_ref.shape, jnp.int32)
    base = base_ref[0]
    for patch in range(patches):
        begin = starts_ref[patch] - base
        first = jnp.where(row == patch, begin, first)
        if patch > 0:
            end = jnp.where(row == patch - 1, begin, end)
    first_ref[...] = first
    end_ref[...] = jnp.where(row == patches - 1, shard_bytes + straddle_ref[0], end)


def own_keys(base, starts, straddle, states, key_weight):
    patches = starts.shape[0]
    bounds = jax.ShapeDtypeStruct((patches, 128), jnp.int32)
    return pl.pallas_call(
        keys_kernel,
        out_shape=(
            jax.ShapeDtypeStruct(states.shape, jnp.bfloat16),
            bounds,
            bounds,
            jax.ShapeDtypeStruct(states.shape, jnp.bfloat16),
            jax.ShapeDtypeStruct(key_weight.shape, jnp.bfloat16),
        ),
        in_specs=scalars(3) + whole(2),
        out_specs=tuple(whole(5)),
        compiler_params=pltpu.CompilerParams(vmem_limit_bytes=8 << 20),
        name="own_keys",
    )(base.reshape(1), starts, straddle, states, key_weight)


def pool_kernel(first_ref, end_ref, states_ref, halo_ref, keys_ref, weight_ref, out_ref):
    window = jnp.concatenate([states_ref[...], halo_ref[...]], axis=0)
    halo_keys = jnp.dot(
        halo_ref[...], weight_ref[...], preferred_element_type=jnp.float32
    ).astype(jnp.bfloat16)
    keys = jnp.concatenate([keys_ref[...], halo_keys], axis=0)
    patches = first_ref.shape[0]
    position = lax.broadcasted_iota(jnp.int32, (patches, window.shape[0]), 1)
    member = (position >= first_ref[:, :1]) & (position < end_ref[:, :1])
    ones = jnp.where(member, jnp.float32(1.0), jnp.float32(0.0))
    byte_count = jnp.sum(ones, axis=1, keepdims=True)
    query = (
        jnp.dot(ones.astype(jnp.bfloat16), window, preferred_element_type=jnp.float32) / byte_count
    ).astype(jnp.bfloat16)
    pooled = []
    for head in range(window.shape[1] // LHD):
        part = slice(head * LHD, (head + 1) * LHD)
        scores = lax.dot_general(
            query[:, part],
            keys[:, part],
            (((1,), (1,)), ((), ())),
            preferred_element_type=jnp.float32,
        ) * jnp.float32(LHD**-0.5)
        scores = jnp.where(member, scores, jnp.float32(-1e30))
        row_peak = jnp.max(scores, axis=1, keepdims=True)
        expo = jnp.where(member, jnp.exp(scores - row_peak), jnp.float32(0.0))
        cross = (expo / jnp.sum(expo, axis=1, keepdims=True)).astype(jnp.bfloat16)
        pooled.append(
            jnp.dot(cross, window[:, part], preferred_element_type=jnp.float32).astype(jnp.bfloat16)
        )
    block = jnp.concatenate(pooled, axis=1)
    for target in range(out_ref.shape[0]):
        out_ref[target] = block


def pool(first, end, states, halo, keys, key_weight, copies):
    patches, width = first.shape[0], states.shape[1]
    return pl.pallas_call(
        pool_kernel,
        out_shape=jax.ShapeDtypeStruct((copies, patches, width), jnp.bfloat16),
        in_specs=whole(6),
        out_specs=pl.BlockSpec(memory_space=pltpu.VMEM),
        compiler_params=pltpu.CompilerParams(vmem_limit_bytes=16 << 20),
        name="pool",
    )(first, end, states, halo, keys, key_weight)


def merge_kernel(blocks_ref, weight_ref, out_ref, total_ref):
    step = pl.program_id(0)

    @pl.when(step == 0)
    def _():
        total_ref[...] = jnp.zeros_like(total_ref)

    rows = jnp.concatenate([blocks_ref[shard] for shard in range(blocks_ref.shape[0])], axis=1)
    for part in range(weight_ref.shape[0]):
        total_ref[:, part * HD : (part + 1) * HD] += jnp.dot(
            rows, weight_ref[part].reshape(rows.shape[1], -1), preferred_element_type=jnp.float32
        )

    @pl.when(step == pl.num_programs(0) - 1)
    def _():
        out_ref[...] = total_ref[...].astype(jnp.bfloat16)


def merge_weights(blocks, attn_weight):
    planes = jnp.swapaxes(attn_weight, 0, 1)
    steps, group, _, columns = blocks.shape
    parts, _, width = planes.shape
    return pl.pallas_call(
        merge_kernel,
        out_shape=jax.ShapeDtypeStruct((ROWS, parts * width), jnp.bfloat16),
        grid=(steps,),
        in_specs=[
            pl.BlockSpec((None, group, ROWS, columns), lambda s: (s, 0, 0, 0)),
            pl.BlockSpec((parts, group, None, columns, width), lambda s: (0, 0, s, 0, 0)),
        ],
        out_specs=pl.BlockSpec((ROWS, parts * width), lambda s: (0, 0)),
        scratch_shapes=[pltpu.VMEM((ROWS, parts * width), jnp.float32)],
        name="merge",
    )(blocks, planes.reshape(parts, group, steps, columns, width))


def attend_kernel(model_width, square_ref, pooled_ref, merged_ref, out_ref, view_ref):
    square = jnp.sum(square_ref[...], axis=0) / jnp.float32(model_width)
    inverse = lax.rsqrt(square + jnp.float32(epsilon))
    diagonal = lax.broadcasted_iota(jnp.int32, (128, 128), 0) == lax.broadcasted_iota(
        jnp.int32, (128, 128), 1
    )
    patches = pooled_ref.shape[0]
    columns = []
    for tile in range(patches // 128):
        spread_row = jnp.broadcast_to(inverse[tile : tile + 1, :], (128, 128))
        columns.append(
            jnp.sum(jnp.where(diagonal, spread_row, jnp.float32(0.0)), axis=1, keepdims=True)
        )
    for tile in range(patches // WIDE):
        rows = slice(tile * WIDE, (tile + 1) * WIDE)
        column = jnp.concatenate(columns[tile * WIDE // 128 : (tile + 1) * WIDE // 128], axis=0)
        view_ref[rows, :] = (
            jnp.dot(pooled_ref[rows, :], merged_ref[...], preferred_element_type=jnp.float32)
            * column
        ).astype(jnp.bfloat16)
    causal = lax.broadcasted_iota(jnp.int32, (TILE, TILE), 0) >= lax.broadcasted_iota(
        jnp.int32, (TILE, TILE), 1
    )
    scale = jnp.float32(HD**-0.5)
    for tile in range(patches // TILE):
        rows = slice(tile * TILE, (tile + 1) * TILE)
        query = view_ref[rows, :HD]

        def against(keys):
            return lax.dot_general(
                query, keys, (((1,), (1,)), ((), ())), preferred_element_type=jnp.float32
            )

        near = jnp.where(causal, against(view_ref[rows, HD : 2 * HD]), jnp.float32(-1e30))
        peak = jnp.max(near, axis=1, keepdims=True)
        if tile > 0:
            far = against(view_ref[: tile * TILE, HD : 2 * HD])
            peak = jnp.maximum(peak, jnp.max(far, axis=1, keepdims=True))
        near = jnp.exp((near - peak) * scale)
        total = jnp.sum(near, axis=1, keepdims=True)
        result = jnp.dot(
            near.astype(jnp.bfloat16), view_ref[rows, 2 * HD :], preferred_element_type=jnp.float32
        )
        if tile > 0:
            far = jnp.exp((far - peak) * scale)
            total = total + jnp.sum(far, axis=1, keepdims=True)
            result = result + jnp.dot(
                far.astype(jnp.bfloat16),
                view_ref[: tile * TILE, 2 * HD :],
                preferred_element_type=jnp.float32,
            )
        out_ref[rows, :] = (result * (jnp.float32(1.0) / total)).astype(jnp.bfloat16)


def attend(model_width, square_all, pooled_all, merged_all):
    patches = pooled_all.shape[0]
    return pl.pallas_call(
        functools.partial(attend_kernel, model_width),
        out_shape=jax.ShapeDtypeStruct((patches, HD), jnp.bfloat16),
        in_specs=whole(3),
        out_specs=pl.BlockSpec(memory_space=pltpu.VMEM),
        scratch_shapes=[pltpu.VMEM((patches, merged_all.shape[1]), jnp.bfloat16)],
        compiler_params=pltpu.CompilerParams(vmem_limit_bytes=24 << 20),
        name="attend",
    )(square_all, pooled_all, merged_all)


def exchange(blocks, axis):
    return lax.all_to_all(blocks, axis, split_axis=0, concat_axis=0, tiled=True)


def layer(states, starts, straddle, key_weight, out_weight, norm_gain, attn_weight):
    seq = lax.axis_size("seq")
    base = lax.axis_index("seq") * states.shape[0]
    model_width = attn_weight.shape[0]
    pooled_width = out_weight.shape[0]
    lines = [list(range(i, i + ALONG_X)) for i in range(0, seq, ALONG_X)]
    columns = [list(range(i, seq, ALONG_X)) for i in range(ALONG_X)]

    row_blocks, edge = weight_rows(
        out_weight, norm_gain, states, lax.axis_index("rep"), seq // ALONG_X
    )
    column_blocks = lax.all_to_all(
        row_blocks, "seq", split_axis=0, concat_axis=0, tiled=True, axis_index_groups=columns
    )
    halo_rows = shifted(edge, "seq", -1)
    keys, first, end, own, weight = own_keys(base, starts, straddle, states, key_weight)
    pooled_blocks = pool(first, end, own, halo_rows, keys, weight, seq)
    pooled_all = exchange(pooled_blocks, "seq").reshape(-1, pooled_width)
    weight_blocks = lax.all_gather(
        column_blocks.reshape(-1, column_blocks.shape[2]),
        "seq",
        axis=0,
        tiled=True,
        axis_index_groups=lines,
    ).reshape(ALONG_X, *column_blocks.shape)
    merged = merge_weights(weight_blocks, attn_weight)
    merged_all = lax.all_gather(merged, "rep", axis=0, tiled=True)
    part = lax.dot_general(
        out_weight, pooled_all, (((0,), (1,)), ((), ())), preferred_element_type=jnp.float32
    )
    part_square = jnp.sum(part * part, axis=0).reshape(-1, 128)
    square_all = exchange(jnp.broadcast_to(part_square[None], (seq,) + part_square.shape), "seq")
    attended = attend(model_width, square_all, pooled_all, merged_all)
    return lax.all_to_all(attended, "seq", split_axis=0, concat_axis=1, tiled=True)


def solution(mesh):
    placed = (
        P(("rep", "seq"), None),
        P(("rep", "seq")),
        P(("rep", "seq")),
        P(),
        P(None, "seq"),
        P("seq"),
        P(None, None, "seq"),
    )
    return jax.shard_map(
        layer, mesh=mesh, in_specs=placed, out_specs=P(("rep", "seq"), None), check_vma=False
    )
```

```python
import functools

import jax
import jax.numpy as jnp
from jax import lax
from jax.experimental import pallas as pl
from jax.experimental.pallas import tpu as pltpu
from jax.sharding import PartitionSpec as P


HD = 128
LHD = 128
HALO = 64
ROWS = 32
TILE = 256
WIDE = 512


epsilon = 1e-05


def shifted(shard, axis, by):
    size = lax.axis_size(axis)
    pairs = [(i, i + by) for i in range(size) if 0 <= i + by < size]
    return lax.ppermute(shard, axis, pairs)


def whole(count):
    return [pl.BlockSpec(memory_space=pltpu.VMEM)] * count


def scalars(count):
    return [pl.BlockSpec(memory_space=pltpu.SMEM)] * count


def rows_kernel(index_ref, weight_ref, gain_ref, states_ref, out_ref, edge_ref):
    block = (weight_ref[...].astype(jnp.float32) * gain_ref[...].astype(jnp.float32)).astype(
        jnp.bfloat16
    )
    for target in range(out_ref.shape[0]):
        out_ref[target] = block
    edge_ref[...] = states_ref[...]


def weight_rows(out_weight, norm_gain, states, index, copies):
    columns, width = out_weight.shape[1], states.shape[1]
    return pl.pallas_call(
        rows_kernel,
        out_shape=(
            jax.ShapeDtypeStruct((copies, ROWS, columns), jnp.bfloat16),
            jax.ShapeDtypeStruct((HALO, width), jnp.bfloat16),
        ),
        grid_spec=pltpu.PrefetchScalarGridSpec(
            num_scalar_prefetch=1,
            grid=(1,),
            in_specs=[
                pl.BlockSpec((ROWS, columns), lambda step, index: (index[0], 0)),
                pl.BlockSpec((1, columns), lambda step, index: (0, 0)),
                pl.BlockSpec((HALO, width), lambda step, index: (0, 0)),
            ],
            out_specs=[
                pl.BlockSpec((copies, ROWS, columns), lambda step, index: (0, 0, 0)),
                pl.BlockSpec((HALO, width), lambda step, index: (0, 0)),
            ],
        ),
        name="rows",
    )(index.reshape(1), out_weight, norm_gain.reshape(1, -1), states)


def keys_kernel(base_ref, starts_ref, straddle_ref, states_ref, weight_ref, keys_ref, first_ref, end_ref, states_out, weight_out):
    patches = first_ref.shape[0]
    shard_bytes = states_ref.shape[0]
    keys_ref[...] = jnp.dot(
        states_ref[...], weight_ref[...], preferred_element_type=jnp.float32
    ).astype(jnp.bfloat16)
    states_out[...] = states_ref[...]
    weight_out[...] = weight_ref[...]
    row = lax.broadcasted_iota(jnp.int32, first_ref.shape, 0)
    first = jnp.zeros(first_ref.shape, jnp.int32)
    end = jnp.zeros(first_ref.shape, jnp.int32)
    base = base_ref[0]
    for patch in range(patches):
        begin = starts_ref[patch] - base
        first = jnp.where(row == patch, begin, first)
        if patch > 0:
            end = jnp.where(row == patch - 1, begin, end)
    first_ref[...] = first
    end_ref[...] = jnp.where(row == patches - 1, shard_bytes + straddle_ref[0], end)


def own_keys(base, starts, straddle, states, key_weight):
    patches = starts.shape[0]
    bounds = jax.ShapeDtypeStruct((patches, 128), jnp.int32)
    return pl.pallas_call(
        keys_kernel,
        out_shape=(
            jax.ShapeDtypeStruct(states.shape, jnp.bfloat16),
            bounds,
            bounds,
            jax.ShapeDtypeStruct(states.shape, jnp.bfloat16),
            jax.ShapeDtypeStruct(key_weight.shape, jnp.bfloat16),
        ),
        in_specs=scalars(3) + whole(2),
        out_specs=tuple(whole(5)),
        compiler_params=pltpu.CompilerParams(vmem_limit_bytes=8 << 20),
        name="own_keys",
    )(base.reshape(1), starts, straddle, states, key_weight)


def pool_kernel(first_ref, end_ref, states_ref, halo_ref, keys_ref, weight_ref, out_ref):
    window = jnp.concatenate([states_ref[...], halo_ref[...]], axis=0)
    halo_keys = jnp.dot(
        halo_ref[...], weight_ref[...], preferred_element_type=jnp.float32
    ).astype(jnp.bfloat16)
    keys = jnp.concatenate([keys_ref[...], halo_keys], axis=0)
    patches = first_ref.shape[0]
    position = lax.broadcasted_iota(jnp.int32, (patches, window.shape[0]), 1)
    member = (position >= first_ref[:, :1]) & (position < end_ref[:, :1])
    ones = jnp.where(member, jnp.float32(1.0), jnp.float32(0.0))
    byte_count = jnp.sum(ones, axis=1, keepdims=True)
    query = (
        jnp.dot(ones.astype(jnp.bfloat16), window, preferred_element_type=jnp.float32) / byte_count
    ).astype(jnp.bfloat16)
    pooled = []
    for head in range(window.shape[1] // LHD):
        part = slice(head * LHD, (head + 1) * LHD)
        scores = lax.dot_general(
            query[:, part],
            keys[:, part],
            (((1,), (1,)), ((), ())),
            preferred_element_type=jnp.float32,
        ) * jnp.float32(LHD**-0.5)
        scores = jnp.where(member, scores, jnp.float32(-1e30))
        row_peak = jnp.max(scores, axis=1, keepdims=True)
        expo = jnp.where(member, jnp.exp(scores - row_peak), jnp.float32(0.0))
        cross = (expo / jnp.sum(expo, axis=1, keepdims=True)).astype(jnp.bfloat16)
        pooled.append(
            jnp.dot(cross, window[:, part], preferred_element_type=jnp.float32).astype(jnp.bfloat16)
        )
    block = jnp.concatenate(pooled, axis=1)
    for target in range(out_ref.shape[0]):
        out_ref[target] = block


def pool(first, end, states, halo, keys, key_weight, copies):
    patches, width = first.shape[0], states.shape[1]
    return pl.pallas_call(
        pool_kernel,
        out_shape=jax.ShapeDtypeStruct((copies, patches, width), jnp.bfloat16),
        in_specs=whole(6),
        out_specs=pl.BlockSpec(memory_space=pltpu.VMEM),
        compiler_params=pltpu.CompilerParams(vmem_limit_bytes=16 << 20),
        name="pool",
    )(first, end, states, halo, keys, key_weight)


def merge_kernel(blocks_ref, weight_ref, out_ref, total_ref):
    step = pl.program_id(0)

    @pl.when(step == 0)
    def _():
        total_ref[...] = jnp.zeros_like(total_ref)

    rows = jnp.concatenate([blocks_ref[shard] for shard in range(blocks_ref.shape[0])], axis=1)
    for part in range(weight_ref.shape[0]):
        total_ref[:, part * HD : (part + 1) * HD] += jnp.dot(
            rows, weight_ref[part], preferred_element_type=jnp.float32
        )

    @pl.when(step == pl.num_programs(0) - 1)
    def _():
        out_ref[...] = total_ref[...].astype(jnp.bfloat16)


def merge_weights(blocks, attn_weight):
    shards_total, block_rows, columns = blocks.shape
    steps = 4
    group = shards_total // steps
    planes = jnp.swapaxes(attn_weight, 0, 1)
    parts, _, width = planes.shape
    return pl.pallas_call(
        merge_kernel,
        out_shape=jax.ShapeDtypeStruct((ROWS, parts * width), jnp.bfloat16),
        grid=(steps,),
        in_specs=[
            pl.BlockSpec((group, block_rows, columns), lambda s: (s, 0, 0)),
            pl.BlockSpec((parts, group * columns, width), lambda s: (0, s, 0)),
        ],
        out_specs=pl.BlockSpec((ROWS, parts * width), lambda s: (0, 0)),
        scratch_shapes=[pltpu.VMEM((ROWS, parts * width), jnp.float32)],
        compiler_params=pltpu.CompilerParams(vmem_limit_bytes=16 << 20),
        name="merge",
    )(blocks, planes)


def attend_kernel(model_width, square_ref, pooled_ref, merged_ref, out_ref, view_ref):
    square = jnp.sum(square_ref[...], axis=0) / jnp.float32(model_width)
    inverse = lax.rsqrt(square + jnp.float32(epsilon))
    diagonal = lax.broadcasted_iota(jnp.int32, (128, 128), 0) == lax.broadcasted_iota(
        jnp.int32, (128, 128), 1
    )
    patches = pooled_ref.shape[0]
    columns = []
    for tile in range(patches // 128):
        spread_row = jnp.broadcast_to(inverse[tile : tile + 1, :], (128, 128))
        columns.append(
            jnp.sum(jnp.where(diagonal, spread_row, jnp.float32(0.0)), axis=1, keepdims=True)
        )
    for tile in range(patches // WIDE):
        rows = slice(tile * WIDE, (tile + 1) * WIDE)
        column = jnp.concatenate(columns[tile * WIDE // 128 : (tile + 1) * WIDE // 128], axis=0)
        view_ref[rows, :] = (
            jnp.dot(pooled_ref[rows, :], merged_ref[...], preferred_element_type=jnp.float32)
            * column
        ).astype(jnp.bfloat16)
    causal = lax.broadcasted_iota(jnp.int32, (TILE, TILE), 0) >= lax.broadcasted_iota(
        jnp.int32, (TILE, TILE), 1
    )
    scale = jnp.float32(HD**-0.5)

    def against(tile, first, last):
        return lax.dot_general(
            view_ref[tile * TILE : (tile + 1) * TILE, :HD],
            view_ref[first * TILE : last * TILE, HD : 2 * HD],
            (((1,), (1,)), ((), ())),
            preferred_element_type=jnp.float32,
        )

    tiles = range(patches // TILE)
    scores = [
        (
            jnp.where(causal, against(tile, tile, tile + 1), jnp.float32(-1e30)),
            against(tile, 0, tile) if tile > 0 else None,
        )
        for tile in tiles
    ]
    for tile, (near, far) in zip(tiles, scores):
        rows = slice(tile * TILE, (tile + 1) * TILE)
        peak = jnp.max(near, axis=1, keepdims=True)
        if tile > 0:
            peak = jnp.maximum(peak, jnp.max(far, axis=1, keepdims=True))
        near = jnp.exp((near - peak) * scale)
        total = jnp.sum(near, axis=1, keepdims=True)
        result = jnp.dot(
            near.astype(jnp.bfloat16), view_ref[rows, 2 * HD :], preferred_element_type=jnp.float32
        )
        if tile > 0:
            far = jnp.exp((far - peak) * scale)
            total = total + jnp.sum(far, axis=1, keepdims=True)
            result = result + jnp.dot(
                far.astype(jnp.bfloat16),
                view_ref[: tile * TILE, 2 * HD :],
                preferred_element_type=jnp.float32,
            )
        out_ref[rows, :] = (result * (jnp.float32(1.0) / total)).astype(jnp.bfloat16)


def attend(model_width, square_all, pooled_all, merged_all):
    patches = pooled_all.shape[0]
    return pl.pallas_call(
        functools.partial(attend_kernel, model_width),
        out_shape=jax.ShapeDtypeStruct((patches, HD), jnp.bfloat16),
        in_specs=whole(3),
        out_specs=pl.BlockSpec(memory_space=pltpu.VMEM),
        scratch_shapes=[pltpu.VMEM((patches, merged_all.shape[1]), jnp.bfloat16)],
        compiler_params=pltpu.CompilerParams(vmem_limit_bytes=24 << 20),
        name="attend",
    )(square_all, pooled_all, merged_all)


def exchange(blocks, axis):
    return lax.all_to_all(blocks, axis, split_axis=0, concat_axis=0, tiled=True)


def layer(states, starts, straddle, key_weight, out_weight, norm_gain, attn_weight):
    seq = lax.axis_size("seq")
    base = lax.axis_index("seq") * states.shape[0]
    model_width = attn_weight.shape[0]
    pooled_width = out_weight.shape[0]

    row_blocks, edge = weight_rows(out_weight, norm_gain, states, lax.axis_index("rep"), seq)
    weight_blocks = exchange(row_blocks, "seq")
    halo_rows = shifted(edge, "seq", -1)
    keys, first, end, own, weight = own_keys(base, starts, straddle, states, key_weight)
    pooled_blocks = pool(first, end, own, halo_rows, keys, weight, seq)
    pooled_all = exchange(pooled_blocks, "seq").reshape(-1, pooled_width)
    merged = merge_weights(weight_blocks, attn_weight)
    merged_all = lax.all_gather(merged, "rep", axis=0, tiled=True)
    part = lax.dot_general(
        out_weight, pooled_all, (((0,), (1,)), ((), ())), preferred_element_type=jnp.float32
    )
    part_square = jnp.sum(part * part, axis=0).reshape(-1, 128)
    square_all = exchange(jnp.broadcast_to(part_square[None], (seq,) + part_square.shape), "seq")
    attended = attend(model_width, square_all, pooled_all, merged_all)
    return lax.all_to_all(attended, "seq", split_axis=0, concat_axis=1, tiled=True)


def solution(mesh):
    placed = (
        P(("rep", "seq"), None),
        P(("rep", "seq")),
        P(("rep", "seq")),
        P(),
        P(None, "seq"),
        P("seq"),
        P(None, None, "seq"),
    )
    return jax.shard_map(
        layer, mesh=mesh, in_specs=placed, out_specs=P(("rep", "seq"), None), check_vma=False
    )
```

```python
import functools

import jax
import jax.numpy as jnp
from jax import lax
from jax.experimental import pallas as pl
from jax.experimental.pallas import tpu as pltpu
from jax.sharding import PartitionSpec as P


HD = 128
LHD = 128
HALO = 64
ROWS = 32
TILE = 256
WIDE = 512


epsilon = 1e-05


def shifted(shard, axis, by):
    size = lax.axis_size(axis)
    pairs = [(i, i + by) for i in range(size) if 0 <= i + by < size]
    return lax.ppermute(shard, axis, pairs)


def whole(count):
    return [pl.BlockSpec(memory_space=pltpu.VMEM)] * count


def scalars(count):
    return [pl.BlockSpec(memory_space=pltpu.SMEM)] * count


def rows_kernel(index_ref, weight_ref, gain_ref, states_ref, out_ref, edge_ref):
    out_ref[...] = (weight_ref[...].astype(jnp.float32) * gain_ref[...].astype(jnp.float32)).astype(
        jnp.bfloat16
    )
    edge_ref[...] = states_ref[...]


def weight_rows(out_weight, norm_gain, states, index):
    columns, width = out_weight.shape[1], states.shape[1]
    return pl.pallas_call(
        rows_kernel,
        out_shape=(
            jax.ShapeDtypeStruct((ROWS, columns), jnp.bfloat16),
            jax.ShapeDtypeStruct((HALO, width), jnp.bfloat16),
        ),
        grid_spec=pltpu.PrefetchScalarGridSpec(
            num_scalar_prefetch=1,
            grid=(1,),
            in_specs=[
                pl.BlockSpec((ROWS, columns), lambda step, index: (index[0], 0)),
                pl.BlockSpec((1, columns), lambda step, index: (0, 0)),
                pl.BlockSpec((HALO, width), lambda step, index: (0, 0)),
            ],
            out_specs=[
                pl.BlockSpec((ROWS, columns), lambda step, index: (0, 0)),
                pl.BlockSpec((HALO, width), lambda step, index: (0, 0)),
            ],
        ),
        name="rows",
    )(index.reshape(1), out_weight, norm_gain.reshape(1, -1), states)


def keys_kernel(base_ref, starts_ref, straddle_ref, states_ref, weight_ref, keys_ref, first_ref, end_ref, states_out, weight_out):
    patches = first_ref.shape[0]
    shard_bytes = states_ref.shape[0]
    keys_ref[...] = jnp.dot(
        states_ref[...], weight_ref[...], preferred_element_type=jnp.float32
    ).astype(jnp.bfloat16)
    states_out[...] = states_ref[...]
    weight_out[...] = weight_ref[...]
    row = lax.broadcasted_iota(jnp.int32, first_ref.shape, 0)
    first = jnp.zeros(first_ref.shape, jnp.int32)
    end = jnp.zeros(first_ref.shape, jnp.int32)
    base = base_ref[0]
    for patch in range(patches):
        begin = starts_ref[patch] - base
        first = jnp.where(row == patch, begin, first)
        if patch > 0:
            end = jnp.where(row == patch - 1, begin, end)
    first_ref[...] = first
    end_ref[...] = jnp.where(row == patches - 1, shard_bytes + straddle_ref[0], end)


def own_keys(base, starts, straddle, states, key_weight):
    patches = starts.shape[0]
    bounds = jax.ShapeDtypeStruct((patches, 128), jnp.int32)
    return pl.pallas_call(
        keys_kernel,
        out_shape=(
            jax.ShapeDtypeStruct(states.shape, jnp.bfloat16),
            bounds,
            bounds,
            jax.ShapeDtypeStruct(states.shape, jnp.bfloat16),
            jax.ShapeDtypeStruct(key_weight.shape, jnp.bfloat16),
        ),
        in_specs=scalars(3) + whole(2),
        out_specs=tuple(whole(5)),
        compiler_params=pltpu.CompilerParams(vmem_limit_bytes=8 << 20),
        name="own_keys",
    )(base.reshape(1), starts, straddle, states, key_weight)


def pool_kernel(first_ref, end_ref, states_ref, halo_ref, keys_ref, weight_ref, rows_ref, out_ref):
    window = jnp.concatenate([states_ref[...], halo_ref[...]], axis=0)
    halo_keys = jnp.dot(
        halo_ref[...], weight_ref[...], preferred_element_type=jnp.float32
    ).astype(jnp.bfloat16)
    keys = jnp.concatenate([keys_ref[...], halo_keys], axis=0)
    patches = first_ref.shape[0]
    position = lax.broadcasted_iota(jnp.int32, (patches, window.shape[0]), 1)
    member = (position >= first_ref[:, :1]) & (position < end_ref[:, :1])
    ones = jnp.where(member, jnp.float32(1.0), jnp.float32(0.0))
    byte_count = jnp.sum(ones, axis=1, keepdims=True)
    query = (
        jnp.dot(ones.astype(jnp.bfloat16), window, preferred_element_type=jnp.float32) / byte_count
    ).astype(jnp.bfloat16)
    pooled = []
    for head in range(window.shape[1] // LHD):
        part = slice(head * LHD, (head + 1) * LHD)
        scores = lax.dot_general(
            query[:, part],
            keys[:, part],
            (((1,), (1,)), ((), ())),
            preferred_element_type=jnp.float32,
        ) * jnp.float32(LHD**-0.5)
        scores = jnp.where(member, scores, jnp.float32(-1e30))
        row_peak = jnp.max(scores, axis=1, keepdims=True)
        expo = jnp.where(member, jnp.exp(scores - row_peak), jnp.float32(0.0))
        cross = (expo / jnp.sum(expo, axis=1, keepdims=True)).astype(jnp.bfloat16)
        pooled.append(
            jnp.dot(cross, window[:, part], preferred_element_type=jnp.float32).astype(jnp.bfloat16)
        )
    block = jnp.concatenate(pooled + [rows_ref[...]], axis=1)
    for target in range(out_ref.shape[0]):
        out_ref[target] = block


def pool(first, end, states, halo, keys, key_weight, rows, copies):
    patches, width = first.shape[0], states.shape[1] + rows.shape[1]
    return pl.pallas_call(
        pool_kernel,
        out_shape=jax.ShapeDtypeStruct((copies, patches, width), jnp.bfloat16),
        in_specs=whole(7),
        out_specs=pl.BlockSpec(memory_space=pltpu.VMEM),
        compiler_params=pltpu.CompilerParams(vmem_limit_bytes=16 << 20),
        name="pool",
    )(first, end, states, halo, keys, key_weight, rows)


def merge_kernel(blocks_ref, weight_ref, out_ref, total_ref):
    step = pl.program_id(0)

    @pl.when(step == 0)
    def _():
        total_ref[...] = jnp.zeros_like(total_ref)

    rows = jnp.concatenate([blocks_ref[shard] for shard in range(blocks_ref.shape[0])], axis=1)
    for part in range(weight_ref.shape[0]):
        total_ref[:, part * HD : (part + 1) * HD] += jnp.dot(
            rows, weight_ref[part], preferred_element_type=jnp.float32
        )

    @pl.when(step == pl.num_programs(0) - 1)
    def _():
        out_ref[...] = total_ref[...].astype(jnp.bfloat16)


def merge_weights(blocks, attn_weight):
    shards_total, _, carried = blocks.shape
    steps = 4
    group = shards_total // steps
    planes = jnp.swapaxes(attn_weight, 0, 1)
    parts, model_width, width = planes.shape
    columns = model_width // shards_total
    last = carried // columns - 1
    return pl.pallas_call(
        merge_kernel,
        out_shape=jax.ShapeDtypeStruct((ROWS, parts * width), jnp.bfloat16),
        grid=(steps,),
        in_specs=[
            pl.BlockSpec((group, ROWS, columns), lambda s: (s, 0, last)),
            pl.BlockSpec((parts, group * columns, width), lambda s: (0, s, 0)),
        ],
        out_specs=pl.BlockSpec((ROWS, parts * width), lambda s: (0, 0)),
        scratch_shapes=[pltpu.VMEM((ROWS, parts * width), jnp.float32)],
        compiler_params=pltpu.CompilerParams(vmem_limit_bytes=16 << 20),
        name="merge",
    )(blocks, planes)


def attend_kernel(model_width, square_ref, pooled_ref, merged_ref, out_ref, view_ref):
    square = jnp.sum(square_ref[...], axis=0) / jnp.float32(model_width)
    inverse = lax.rsqrt(square + jnp.float32(epsilon))
    diagonal = lax.broadcasted_iota(jnp.int32, (128, 128), 0) == lax.broadcasted_iota(
        jnp.int32, (128, 128), 1
    )
    patches = pooled_ref.shape[0]
    columns = []
    for tile in range(patches // 128):
        spread_row = jnp.broadcast_to(inverse[tile : tile + 1, :], (128, 128))
        columns.append(
            jnp.sum(jnp.where(diagonal, spread_row, jnp.float32(0.0)), axis=1, keepdims=True)
        )
    for tile in range(patches // WIDE):
        rows = slice(tile * WIDE, (tile + 1) * WIDE)
        column = jnp.concatenate(columns[tile * WIDE // 128 : (tile + 1) * WIDE // 128], axis=0)
        view_ref[rows, :] = (
            jnp.dot(
                pooled_ref[rows, : merged_ref.shape[0]], merged_ref[...], preferred_element_type=jnp.float32)
            * column
        ).astype(jnp.bfloat16)
    causal = lax.broadcasted_iota(jnp.int32, (TILE, TILE), 0) >= lax.broadcasted_iota(
        jnp.int32, (TILE, TILE), 1
    )
    scale = jnp.float32(HD**-0.5)

    def against(tile, first, last):
        return lax.dot_general(
            view_ref[tile * TILE : (tile + 1) * TILE, :HD],
            view_ref[first * TILE : last * TILE, HD : 2 * HD],
            (((1,), (1,)), ((), ())),
            preferred_element_type=jnp.float32,
        )

    tiles = range(patches // TILE)
    scores = [
        (
            jnp.where(causal, against(tile, tile, tile + 1), jnp.float32(-1e30)),
            against(tile, 0, tile) if tile > 0 else None,
        )
        for tile in tiles
    ]
    for tile, (near, far) in zip(tiles, scores):
        rows = slice(tile * TILE, (tile + 1) * TILE)
        peak = jnp.max(near, axis=1, keepdims=True)
        if tile > 0:
            peak = jnp.maximum(peak, jnp.max(far, axis=1, keepdims=True))
        near = jnp.exp((near - peak) * scale)
        total = jnp.sum(near, axis=1, keepdims=True)
        result = jnp.dot(
            near.astype(jnp.bfloat16), view_ref[rows, 2 * HD :], preferred_element_type=jnp.float32
        )
        if tile > 0:
            far = jnp.exp((far - peak) * scale)
            total = total + jnp.sum(far, axis=1, keepdims=True)
            result = result + jnp.dot(
                far.astype(jnp.bfloat16),
                view_ref[: tile * TILE, 2 * HD :],
                preferred_element_type=jnp.float32,
            )
        out_ref[rows, :] = (result * (jnp.float32(1.0) / total)).astype(jnp.bfloat16)


def attend(model_width, square_all, pooled_all, merged_all):
    patches = pooled_all.shape[0]
    return pl.pallas_call(
        functools.partial(attend_kernel, model_width),
        out_shape=jax.ShapeDtypeStruct((patches, HD), jnp.bfloat16),
        in_specs=whole(3),
        out_specs=pl.BlockSpec(memory_space=pltpu.VMEM),
        scratch_shapes=[pltpu.VMEM((patches, merged_all.shape[1]), jnp.bfloat16)],
        compiler_params=pltpu.CompilerParams(vmem_limit_bytes=24 << 20),
        name="attend",
    )(square_all, pooled_all, merged_all)


def exchange(blocks, axis):
    return lax.all_to_all(blocks, axis, split_axis=0, concat_axis=0, tiled=True)


def layer(states, starts, straddle, key_weight, out_weight, norm_gain, attn_weight):
    seq = lax.axis_size("seq")
    base = lax.axis_index("seq") * states.shape[0]
    model_width = attn_weight.shape[0]
    pooled_width = out_weight.shape[0]

    rows, edge = weight_rows(out_weight, norm_gain, states, lax.axis_index("rep"))
    halo_rows = shifted(edge, "seq", -1)
    keys, first, end, own, weight = own_keys(base, starts, straddle, states, key_weight)
    blocks = pool(first, end, own, halo_rows, keys, weight, rows, seq)
    blocks = exchange(blocks, "seq")
    carried = blocks.reshape(-1, blocks.shape[2])
    padded = jnp.pad(out_weight, ((0, carried.shape[1] - pooled_width), (0, 0)))
    part = lax.dot_general(
        padded, carried, (((0,), (1,)), ((), ())), preferred_element_type=jnp.float32
    )
    part_square = jnp.sum(part * part, axis=0).reshape(-1, 128)
    square_all = exchange(jnp.broadcast_to(part_square[None], (seq,) + part_square.shape), "seq")
    merged = merge_weights(blocks, attn_weight)
    merged_all = lax.all_gather(merged, "rep", axis=0, tiled=True)
    attended = attend(model_width, square_all, carried, merged_all)
    return lax.all_to_all(attended, "seq", split_axis=0, concat_axis=1, tiled=True)


def solution(mesh):
    placed = (
        P(("rep", "seq"), None),
        P(("rep", "seq")),
        P(("rep", "seq")),
        P(),
        P(None, "seq"),
        P("seq"),
        P(None, None, "seq"),
    )
    return jax.shard_map(
        layer, mesh=mesh, in_specs=placed, out_specs=P(("rep", "seq"), None), check_vma=False
    )
```

```python
import functools

import jax
import jax.numpy as jnp
from jax import lax
from jax.experimental import pallas as pl
from jax.experimental.pallas import tpu as pltpu
from jax.sharding import PartitionSpec as P


HD = 128
LHD = 128
HALO = 64
ROWS = 32
TILE = 256
WIDE = 512


epsilon = 1e-05


def shifted(shard, axis, by):
    size = lax.axis_size(axis)
    pairs = [(i, i + by) for i in range(size) if 0 <= i + by < size]
    return lax.ppermute(shard, axis, pairs)


def whole(count):
    return [pl.BlockSpec(memory_space=pltpu.VMEM)] * count


def scalars(count):
    return [pl.BlockSpec(memory_space=pltpu.SMEM)] * count


def rows_kernel(index_ref, weight_ref, gain_ref, states_ref, out_ref, edge_ref):
    block = (weight_ref[...].astype(jnp.float32) * gain_ref[...].astype(jnp.float32)).astype(
        jnp.bfloat16
    )
    for target in range(out_ref.shape[0]):
        out_ref[target] = block
    edge_ref[...] = states_ref[...]


def weight_rows(out_weight, norm_gain, states, index, copies):
    columns, width = out_weight.shape[1], states.shape[1]
    return pl.pallas_call(
        rows_kernel,
        out_shape=(
            jax.ShapeDtypeStruct((copies, ROWS, columns), jnp.bfloat16),
            jax.ShapeDtypeStruct((HALO, width), jnp.bfloat16),
        ),
        grid_spec=pltpu.PrefetchScalarGridSpec(
            num_scalar_prefetch=1,
            grid=(1,),
            in_specs=[
                pl.BlockSpec((ROWS, columns), lambda step, index: (index[0], 0)),
                pl.BlockSpec((1, columns), lambda step, index: (0, 0)),
                pl.BlockSpec((HALO, width), lambda step, index: (0, 0)),
            ],
            out_specs=[
                pl.BlockSpec((copies, ROWS, columns), lambda step, index: (0, 0, 0)),
                pl.BlockSpec((HALO, width), lambda step, index: (0, 0)),
            ],
        ),
        name="rows",
    )(index.reshape(1), out_weight, norm_gain.reshape(1, -1), states)


def keys_kernel(base_ref, starts_ref, straddle_ref, states_ref, weight_ref, keys_ref, first_ref, end_ref, states_out, weight_out):
    patches = first_ref.shape[0]
    shard_bytes = states_ref.shape[0]
    keys_ref[...] = jnp.dot(
        states_ref[...], weight_ref[...], preferred_element_type=jnp.float32
    ).astype(jnp.bfloat16)
    states_out[...] = states_ref[...]
    weight_out[...] = weight_ref[...]
    row = lax.broadcasted_iota(jnp.int32, first_ref.shape, 0)
    first = jnp.zeros(first_ref.shape, jnp.int32)
    end = jnp.zeros(first_ref.shape, jnp.int32)
    base = base_ref[0]
    for patch in range(patches):
        begin = starts_ref[patch] - base
        first = jnp.where(row == patch, begin, first)
        if patch > 0:
            end = jnp.where(row == patch - 1, begin, end)
    first_ref[...] = first
    end_ref[...] = jnp.where(row == patches - 1, shard_bytes + straddle_ref[0], end)


def own_keys(base, starts, straddle, states, key_weight):
    patches = starts.shape[0]
    bounds = jax.ShapeDtypeStruct((patches, 128), jnp.int32)
    return pl.pallas_call(
        keys_kernel,
        out_shape=(
            jax.ShapeDtypeStruct(states.shape, jnp.bfloat16),
            bounds,
            bounds,
            jax.ShapeDtypeStruct(states.shape, jnp.bfloat16),
            jax.ShapeDtypeStruct(key_weight.shape, jnp.bfloat16),
        ),
        in_specs=scalars(3) + whole(2),
        out_specs=tuple(whole(5)),
        compiler_params=pltpu.CompilerParams(vmem_limit_bytes=8 << 20),
        name="own_keys",
    )(base.reshape(1), starts, straddle, states, key_weight)


def pool_kernel(first_ref, end_ref, states_ref, halo_ref, keys_ref, weight_ref, out_ref):
    window = jnp.concatenate([states_ref[...], halo_ref[...]], axis=0)
    halo_keys = jnp.dot(
        halo_ref[...], weight_ref[...], preferred_element_type=jnp.float32
    ).astype(jnp.bfloat16)
    keys = jnp.concatenate([keys_ref[...], halo_keys], axis=0)
    patches = first_ref.shape[0]
    position = lax.broadcasted_iota(jnp.int32, (patches, window.shape[0]), 1)
    member = (position >= first_ref[:, :1]) & (position < end_ref[:, :1])
    ones = jnp.where(member, jnp.float32(1.0), jnp.float32(0.0))
    byte_count = jnp.sum(ones, axis=1, keepdims=True)
    query = (
        jnp.dot(ones.astype(jnp.bfloat16), window, preferred_element_type=jnp.float32) / byte_count
    ).astype(jnp.bfloat16)
    pooled = []
    for head in range(window.shape[1] // LHD):
        part = slice(head * LHD, (head + 1) * LHD)
        scores = lax.dot_general(
            query[:, part],
            keys[:, part],
            (((1,), (1,)), ((), ())),
            preferred_element_type=jnp.float32,
        ) * jnp.float32(LHD**-0.5)
        scores = jnp.where(member, scores, jnp.float32(-1e30))
        row_peak = jnp.max(scores, axis=1, keepdims=True)
        expo = jnp.where(member, jnp.exp(scores - row_peak), jnp.float32(0.0))
        cross = (expo / jnp.sum(expo, axis=1, keepdims=True)).astype(jnp.bfloat16)
        pooled.append(
            jnp.dot(cross, window[:, part], preferred_element_type=jnp.float32).astype(jnp.bfloat16)
        )
    block = jnp.concatenate(pooled, axis=1)
    for target in range(out_ref.shape[0]):
        out_ref[target] = block


def pool(first, end, states, halo, keys, key_weight, copies):
    patches, width = first.shape[0], states.shape[1]
    return pl.pallas_call(
        pool_kernel,
        out_shape=jax.ShapeDtypeStruct((copies, patches, width), jnp.bfloat16),
        in_specs=whole(6),
        out_specs=pl.BlockSpec(memory_space=pltpu.VMEM),
        compiler_params=pltpu.CompilerParams(vmem_limit_bytes=16 << 20),
        name="pool",
    )(first, end, states, halo, keys, key_weight)


def merge_kernel(blocks_ref, weight_ref, out_ref, total_ref):
    step = pl.program_id(0)

    @pl.when(step == 0)
    def _():
        total_ref[...] = jnp.zeros_like(total_ref)

    rows = jnp.concatenate([blocks_ref[shard] for shard in range(blocks_ref.shape[0])], axis=1)
    for part in range(weight_ref.shape[0]):
        total_ref[:, part * HD : (part + 1) * HD] += jnp.dot(
            rows, weight_ref[part], preferred_element_type=jnp.float32
        )

    @pl.when(step == pl.num_programs(0) - 1)
    def _():
        out_ref[...] = total_ref[...].astype(jnp.bfloat16)


def merge_weights(blocks, attn_weight):
    shards_total, block_rows, columns = blocks.shape
    steps = 4
    group = shards_total // steps
    planes = jnp.swapaxes(attn_weight, 0, 1)
    parts, _, width = planes.shape
    return pl.pallas_call(
        merge_kernel,
        out_shape=jax.ShapeDtypeStruct((ROWS, parts * width), jnp.bfloat16),
        grid=(steps,),
        in_specs=[
            pl.BlockSpec((group, block_rows, columns), lambda s: (s, 0, 0)),
            pl.BlockSpec((parts, group * columns, width), lambda s: (0, s, 0)),
        ],
        out_specs=pl.BlockSpec((ROWS, parts * width), lambda s: (0, 0)),
        scratch_shapes=[pltpu.VMEM((ROWS, parts * width), jnp.float32)],
        compiler_params=pltpu.CompilerParams(vmem_limit_bytes=16 << 20),
        name="merge",
    )(blocks, planes)


def attend_kernel(model_width, square_ref, pooled_ref, merged_ref, out_ref, view_ref):
    square = jnp.sum(square_ref[...], axis=0) / jnp.float32(model_width)
    inverse = lax.rsqrt(square + jnp.float32(epsilon))
    diagonal = lax.broadcasted_iota(jnp.int32, (128, 128), 0) == lax.broadcasted_iota(
        jnp.int32, (128, 128), 1
    )
    patches = pooled_ref.shape[0]
    columns = []
    for tile in range(patches // 128):
        spread_row = jnp.broadcast_to(inverse[tile : tile + 1, :], (128, 128))
        columns.append(
            jnp.sum(jnp.where(diagonal, spread_row, jnp.float32(0.0)), axis=1, keepdims=True)
        )
    for tile in range(patches // WIDE):
        rows = slice(tile * WIDE, (tile + 1) * WIDE)
        column = jnp.concatenate(columns[tile * WIDE // 128 : (tile + 1) * WIDE // 128], axis=0)
        view_ref[rows, :] = (
            jnp.dot(pooled_ref[rows, :], merged_ref[...], preferred_element_type=jnp.float32)
            * column
        ).astype(jnp.bfloat16)
    causal = lax.broadcasted_iota(jnp.int32, (TILE, TILE), 0) >= lax.broadcasted_iota(
        jnp.int32, (TILE, TILE), 1
    )
    scale = jnp.float32(HD**-0.5)

    def against(tile, first, last):
        return lax.dot_general(
            view_ref[tile * TILE : (tile + 1) * TILE, :HD],
            view_ref[first * TILE : last * TILE, HD : 2 * HD],
            (((1,), (1,)), ((), ())),
            preferred_element_type=jnp.float32,
        )

    tiles = range(patches // TILE)
    scores = [
        (
            jnp.where(causal, against(tile, tile, tile + 1), jnp.float32(-1e30)),
            against(tile, 0, tile) if tile > 0 else None,
        )
        for tile in tiles
    ]
    for tile, (near, far) in zip(tiles, scores):
        rows = slice(tile * TILE, (tile + 1) * TILE)
        peak = jnp.max(near, axis=1, keepdims=True)
        if tile > 0:
            peak = jnp.maximum(peak, jnp.max(far, axis=1, keepdims=True))
        near = jnp.exp((near - peak) * scale)
        total = jnp.sum(near, axis=1, keepdims=True)
        result = jnp.dot(
            near.astype(jnp.bfloat16), view_ref[rows, 2 * HD :], preferred_element_type=jnp.float32
        )
        if tile > 0:
            far = jnp.exp((far - peak) * scale)
            total = total + jnp.sum(far, axis=1, keepdims=True)
            result = result + jnp.dot(
                far.astype(jnp.bfloat16),
                view_ref[: tile * TILE, 2 * HD :],
                preferred_element_type=jnp.float32,
            )
        out_ref[rows, :] = (result * (jnp.float32(1.0) / total)).astype(jnp.bfloat16)


def attend(model_width, square_all, pooled_all, merged_all):
    patches = pooled_all.shape[0]
    return pl.pallas_call(
        functools.partial(attend_kernel, model_width),
        out_shape=jax.ShapeDtypeStruct((patches, HD), jnp.bfloat16),
        in_specs=whole(3),
        out_specs=pl.BlockSpec(memory_space=pltpu.VMEM),
        scratch_shapes=[pltpu.VMEM((patches, merged_all.shape[1]), jnp.bfloat16)],
        compiler_params=pltpu.CompilerParams(vmem_limit_bytes=24 << 20),
        name="attend",
    )(square_all, pooled_all, merged_all)


def exchange(blocks, axis, groups=None):
    return lax.all_to_all(
        blocks, axis, split_axis=0, concat_axis=0, tiled=True, axis_index_groups=groups
    )


def scattered(size):
    order = [0]
    while len(order) < size:
        order = [2 * i for i in order] + [2 * i + 1 for i in order]
    return order


def layer(states, starts, straddle, key_weight, out_weight, norm_gain, attn_weight):
    seq = lax.axis_size("seq")
    base = lax.axis_index("seq") * states.shape[0]
    model_width = attn_weight.shape[0]
    pooled_width = out_weight.shape[0]

    row_blocks, edge = weight_rows(out_weight, norm_gain, states, lax.axis_index("rep"), seq)
    weight_blocks = exchange(row_blocks, "seq")
    halo_rows = shifted(edge, "seq", -1)
    keys, first, end, own, weight = own_keys(base, starts, straddle, states, key_weight)
    pooled_blocks = pool(first, end, own, halo_rows, keys, weight, seq)
    pooled_all = exchange(pooled_blocks, "seq").reshape(-1, pooled_width)
    merged = merge_weights(weight_blocks, attn_weight)
    merged_all = lax.all_gather(merged, "rep", axis=0, tiled=True)
    part = lax.dot_general(
        out_weight, pooled_all, (((0,), (1,)), ((), ())), preferred_element_type=jnp.float32
    )
    part_square = jnp.sum(part * part, axis=0).reshape(-1, 128)
    copies = jnp.broadcast_to(part_square[None], (seq,) + part_square.shape)
    square_all = exchange(copies, "seq", [scattered(seq)])
    attended = attend(model_width, square_all, pooled_all, merged_all)
    return lax.all_to_all(attended, "seq", split_axis=0, concat_axis=1, tiled=True)


def solution(mesh):
    placed = (
        P(("rep", "seq"), None),
        P(("rep", "seq")),
        P(("rep", "seq")),
        P(),
        P(None, "seq"),
        P("seq"),
        P(None, None, "seq"),
    )
    return jax.shard_map(
        layer, mesh=mesh, in_specs=placed, out_specs=P(("rep", "seq"), None), check_vma=False
    )
```

```python
import functools

import jax
import jax.numpy as jnp
from jax import lax
from jax.experimental import pallas as pl
from jax.experimental.pallas import tpu as pltpu
from jax.sharding import PartitionSpec as P


HD = 128
LHD = 128
HALO = 64
ROWS = 32
TILE = 256
WIDE = 512


epsilon = 1e-05


def shifted(shard, axis, by):
    size = lax.axis_size(axis)
    pairs = [(i, i + by) for i in range(size) if 0 <= i + by < size]
    return lax.ppermute(shard, axis, pairs)


def whole(count):
    return [pl.BlockSpec(memory_space=pltpu.VMEM)] * count


def scalars(count):
    return [pl.BlockSpec(memory_space=pltpu.SMEM)] * count


def rows_kernel(index_ref, weight_ref, gain_ref, states_ref, out_ref, edge_ref):
    block = (weight_ref[...].astype(jnp.float32) * gain_ref[...].astype(jnp.float32)).astype(
        jnp.bfloat16
    )
    for target in range(out_ref.shape[0]):
        out_ref[target] = block
    edge_ref[...] = states_ref[...]


def weight_rows(out_weight, norm_gain, states, index, copies):
    columns, width = out_weight.shape[1], states.shape[1]
    return pl.pallas_call(
        rows_kernel,
        out_shape=(
            jax.ShapeDtypeStruct((copies, ROWS, columns), jnp.bfloat16),
            jax.ShapeDtypeStruct((HALO, width), jnp.bfloat16),
        ),
        grid_spec=pltpu.PrefetchScalarGridSpec(
            num_scalar_prefetch=1,
            grid=(1,),
            in_specs=[
                pl.BlockSpec((ROWS, columns), lambda step, index: (index[0], 0)),
                pl.BlockSpec((1, columns), lambda step, index: (0, 0)),
                pl.BlockSpec((HALO, width), lambda step, index: (0, 0)),
            ],
            out_specs=[
                pl.BlockSpec((copies, ROWS, columns), lambda step, index: (0, 0, 0)),
                pl.BlockSpec((HALO, width), lambda step, index: (0, 0)),
            ],
        ),
        name="rows",
    )(index.reshape(1), out_weight, norm_gain.reshape(1, -1), states)


def keys_kernel(base_ref, starts_ref, straddle_ref, states_ref, weight_ref, keys_ref, first_ref, end_ref, states_out, weight_out):
    patches = first_ref.shape[0]
    shard_bytes = states_ref.shape[0]
    keys_ref[...] = jnp.dot(
        states_ref[...], weight_ref[...], preferred_element_type=jnp.float32
    ).astype(jnp.bfloat16)
    states_out[...] = states_ref[...]
    weight_out[...] = weight_ref[...]
    row = lax.broadcasted_iota(jnp.int32, first_ref.shape, 0)
    first = jnp.zeros(first_ref.shape, jnp.int32)
    end = jnp.zeros(first_ref.shape, jnp.int32)
    base = base_ref[0]
    for patch in range(patches):
        begin = starts_ref[patch] - base
        first = jnp.where(row == patch, begin, first)
        if patch > 0:
            end = jnp.where(row == patch - 1, begin, end)
    first_ref[...] = first
    end_ref[...] = jnp.where(row == patches - 1, shard_bytes + straddle_ref[0], end)


def own_keys(base, starts, straddle, states, key_weight):
    patches = starts.shape[0]
    bounds = jax.ShapeDtypeStruct((patches, 128), jnp.int32)
    return pl.pallas_call(
        keys_kernel,
        out_shape=(
            jax.ShapeDtypeStruct(states.shape, jnp.bfloat16),
            bounds,
            bounds,
            jax.ShapeDtypeStruct(states.shape, jnp.bfloat16),
            jax.ShapeDtypeStruct(key_weight.shape, jnp.bfloat16),
        ),
        in_specs=scalars(3) + whole(2),
        out_specs=tuple(whole(5)),
        compiler_params=pltpu.CompilerParams(vmem_limit_bytes=8 << 20),
        name="own_keys",
    )(base.reshape(1), starts, straddle, states, key_weight)


def pool_kernel(first_ref, end_ref, states_ref, halo_ref, keys_ref, weight_ref, out_ref):
    window = jnp.concatenate([states_ref[...], halo_ref[...]], axis=0)
    halo_keys = jnp.dot(
        halo_ref[...], weight_ref[...], preferred_element_type=jnp.float32
    ).astype(jnp.bfloat16)
    keys = jnp.concatenate([keys_ref[...], halo_keys], axis=0)
    patches = first_ref.shape[0]
    position = lax.broadcasted_iota(jnp.int32, (patches, window.shape[0]), 1)
    member = (position >= first_ref[:, :1]) & (position < end_ref[:, :1])
    ones = jnp.where(member, jnp.float32(1.0), jnp.float32(0.0))
    byte_count = jnp.sum(ones, axis=1, keepdims=True)
    query = (
        jnp.dot(ones.astype(jnp.bfloat16), window, preferred_element_type=jnp.float32) / byte_count
    ).astype(jnp.bfloat16)
    pooled = []
    for head in range(window.shape[1] // LHD):
        part = slice(head * LHD, (head + 1) * LHD)
        scores = lax.dot_general(
            query[:, part],
            keys[:, part],
            (((1,), (1,)), ((), ())),
            preferred_element_type=jnp.float32,
        ) * jnp.float32(LHD**-0.5)
        scores = jnp.where(member, scores, jnp.float32(-1e30))
        row_peak = jnp.max(scores, axis=1, keepdims=True)
        expo = jnp.where(member, jnp.exp(scores - row_peak), jnp.float32(0.0))
        cross = (expo / jnp.sum(expo, axis=1, keepdims=True)).astype(jnp.bfloat16)
        pooled.append(
            jnp.dot(cross, window[:, part], preferred_element_type=jnp.float32).astype(jnp.bfloat16)
        )
    block = jnp.concatenate(pooled, axis=1)
    for target in range(out_ref.shape[0]):
        out_ref[target] = block


def pool(first, end, states, halo, keys, key_weight, copies):
    patches, width = first.shape[0], states.shape[1]
    return pl.pallas_call(
        pool_kernel,
        out_shape=jax.ShapeDtypeStruct((copies, patches, width), jnp.bfloat16),
        in_specs=whole(6),
        out_specs=pl.BlockSpec(memory_space=pltpu.VMEM),
        compiler_params=pltpu.CompilerParams(vmem_limit_bytes=16 << 20),
        name="pool",
    )(first, end, states, halo, keys, key_weight)


def merge_kernel(order, blocks_ref, weight_ref, out_ref):
    rows = jnp.concatenate([blocks_ref[order.index(shard)] for shard in range(len(order))], axis=1)
    for part in range(weight_ref.shape[0]):
        out_ref[:, part * HD : (part + 1) * HD] = jnp.dot(
            rows, weight_ref[part], preferred_element_type=jnp.float32
        ).astype(jnp.bfloat16)


def merge_weights(blocks, attn_weight):
    planes = jnp.swapaxes(attn_weight, 0, 1)
    parts, _, width = planes.shape
    return pl.pallas_call(
        functools.partial(merge_kernel, scattered(blocks.shape[0])),
        out_shape=jax.ShapeDtypeStruct((ROWS, parts * width), jnp.bfloat16),
        in_specs=whole(2),
        out_specs=pl.BlockSpec(memory_space=pltpu.VMEM),
        compiler_params=pltpu.CompilerParams(vmem_limit_bytes=16 << 20),
        name="merge",
    )(blocks, planes)


def attend_kernel(model_width, square_ref, pooled_ref, merged_ref, out_ref, view_ref):
    square = jnp.sum(square_ref[...], axis=0) / jnp.float32(model_width)
    inverse = lax.rsqrt(square + jnp.float32(epsilon))
    diagonal = lax.broadcasted_iota(jnp.int32, (128, 128), 0) == lax.broadcasted_iota(
        jnp.int32, (128, 128), 1
    )
    patches = pooled_ref.shape[0]
    columns = []
    for tile in range(patches // 128):
        spread_row = jnp.broadcast_to(inverse[tile : tile + 1, :], (128, 128))
        columns.append(
            jnp.sum(jnp.where(diagonal, spread_row, jnp.float32(0.0)), axis=1, keepdims=True)
        )
    for tile in range(patches // WIDE):
        rows = slice(tile * WIDE, (tile + 1) * WIDE)
        column = jnp.concatenate(columns[tile * WIDE // 128 : (tile + 1) * WIDE // 128], axis=0)
        view_ref[rows, :] = (
            jnp.dot(pooled_ref[rows, :], merged_ref[...], preferred_element_type=jnp.float32)
            * column
        ).astype(jnp.bfloat16)
    causal = lax.broadcasted_iota(jnp.int32, (TILE, TILE), 0) >= lax.broadcasted_iota(
        jnp.int32, (TILE, TILE), 1
    )
    scale = jnp.float32(HD**-0.5)
    def against(tile, first, last):
        return lax.dot_general(
            view_ref[tile * TILE : (tile + 1) * TILE, :HD],
            view_ref[first * TILE : last * TILE, HD : 2 * HD],
            (((1,), (1,)), ((), ())),
            preferred_element_type=jnp.float32,
        )

    tiles = range(patches // TILE)
    scores = [
        (
            jnp.where(causal, against(tile, tile, tile + 1), jnp.float32(-1e30)),
            against(tile, 0, tile) if tile > 0 else None,
        )
        for tile in tiles
    ]
    for tile, (near, far) in zip(tiles, scores):
        rows = slice(tile * TILE, (tile + 1) * TILE)
        peak = jnp.max(near, axis=1, keepdims=True)
        if tile > 0:
            peak = jnp.maximum(peak, jnp.max(far, axis=1, keepdims=True))
        near = jnp.exp((near - peak) * scale)
        total = jnp.sum(near, axis=1, keepdims=True)
        result = jnp.dot(
            near.astype(jnp.bfloat16), view_ref[rows, 2 * HD :], preferred_element_type=jnp.float32
        )
        if tile > 0:
            far = jnp.exp((far - peak) * scale)
            total = total + jnp.sum(far, axis=1, keepdims=True)
            result = result + jnp.dot(
                far.astype(jnp.bfloat16),
                view_ref[: tile * TILE, 2 * HD :],
                preferred_element_type=jnp.float32,
            )
        out_ref[rows, :] = (result * (jnp.float32(1.0) / total)).astype(jnp.bfloat16)


def attend(model_width, square_all, pooled_all, merged_all):
    patches = pooled_all.shape[0]
    return pl.pallas_call(
        functools.partial(attend_kernel, model_width),
        out_shape=jax.ShapeDtypeStruct((patches, HD), jnp.bfloat16),
        in_specs=whole(3),
        out_specs=pl.BlockSpec(memory_space=pltpu.VMEM),
        scratch_shapes=[pltpu.VMEM((patches, merged_all.shape[1]), jnp.bfloat16)],
        compiler_params=pltpu.CompilerParams(vmem_limit_bytes=24 << 20),
        name="attend",
    )(square_all, pooled_all, merged_all)


def exchange(blocks, axis, groups=None):
    return lax.all_to_all(
        blocks, axis, split_axis=0, concat_axis=0, tiled=True, axis_index_groups=groups
    )


def scattered(size):
    order = [0]
    while len(order) < size:
        order = [2 * i for i in order] + [2 * i + 1 for i in order]
    return order


def layer(states, starts, straddle, key_weight, out_weight, norm_gain, attn_weight):
    seq = lax.axis_size("seq")
    base = lax.axis_index("seq") * states.shape[0]
    model_width = attn_weight.shape[0]
    pooled_width = out_weight.shape[0]

    row_blocks, edge = weight_rows(out_weight, norm_gain, states, lax.axis_index("rep"), seq)
    weight_blocks = exchange(row_blocks, "seq", [scattered(seq)])
    halo_rows = shifted(edge, "seq", -1)
    keys, first, end, own, weight = own_keys(base, starts, straddle, states, key_weight)
    pooled_blocks = pool(first, end, own, halo_rows, keys, weight, seq)
    pooled_all = exchange(pooled_blocks, "seq").reshape(-1, pooled_width)
    merged = merge_weights(weight_blocks, attn_weight)
    merged_all = lax.all_gather(merged, "rep", axis=0, tiled=True)
    part = lax.dot_general(
        out_weight, pooled_all, (((0,), (1,)), ((), ())), preferred_element_type=jnp.float32
    )
    part_square = jnp.sum(part * part, axis=0).reshape(-1, 128)
    copies = jnp.broadcast_to(part_square[None], (seq,) + part_square.shape)
    square_all = exchange(copies, "seq")
    attended = attend(model_width, square_all, pooled_all, merged_all)
    return lax.all_to_all(attended, "seq", split_axis=0, concat_axis=1, tiled=True)


def solution(mesh):
    placed = (
        P(("rep", "seq"), None),
        P(("rep", "seq")),
        P(("rep", "seq")),
        P(),
        P(None, "seq"),
        P("seq"),
        P(None, None, "seq"),
    )
    return jax.shard_map(
        layer, mesh=mesh, in_specs=placed, out_specs=P(("rep", "seq"), None), check_vma=False
    )
```
